128 devices in a mesh: panel: 8 (over y, core), blk: 16 (over z, x).
Axes of the slice: x: 4, y: 4, z: 4, core: 2. Of those that a mesh axis runs over, the one named last changes fastest.
Arguments:
- source_flux: bfloat16 [72, 512, 2048], P(None, 'panel', 'blk'), may hold values from -6 to 6
- gauss_weight: float32 [4, 2048, 512], P(None, ('panel', 'blk')), may hold values from 0.02 to 0.2
- gauss_offset: float32 [2, 4, 2048, 512], P(None, None, ('panel', 'blk')), may hold values from -0.5 to 0.5
- slot_count: int32 [2048], P(('panel', 'blk')), may hold values from 1 to 512, as said below
- source_cell: int32 [2048, 512], P(('panel', 'blk')), may hold values from 0 to 8191, as said below
- target_cell: int32 [2048, 512], P(('panel', 'blk')), may hold values from 0 to 4095, as said below
- target_area: float32 [524288], P(('panel', 'blk')), may hold values from 0.25 to 1
Outputs:
- remapped: bfloat16 [72, 524288], P(None, ('panel', 'blk'))
The draws below stay inside these ranges and needn't reach their ends.
Inputs may be any that keep to these rules, and one draw needn't show every extreme that they name: `slot_count`: live slots from source s to owner k of its band at entry s * size of blk + k; in every draw some owner receives 512 live slots from every source device of its band. `source_cell`: Row-major index of a cell in the sender's block of 64 x 128; slots past the count hold arbitrary cells. `target_cell`: cell index within owner d's 4096 cells; row d * size of blk + k lists the slots from source k of d's band.
All inputs are finite; a program needn't handle non-finite values.
Results may differ from the reference program's by a relative error of at most 0.0044.
The reference program's roundings to bfloat16 on the way count: a program that leaves them out, or rounds other values in their place, can miss the bound.
Values may be sent and summed in bfloat16 or wider, within the bound.
No kernel may reach another device: no remote copies, remote signals or barrier semaphores. Data moves between devices by JAX's collectives and lax.ppermute only.
A program may use at most 192 MiB of HBM per device.

```python
import math
import jax
import jax.numpy as jnp
from jax import lax

F = 72
Q = 4
SX = 64
SY = 128
OWNERS = 128
CAP = 512
TC = 4096
NSX = 512
NSY = 2048
N_PANEL = 8
N_BLK = 16


def draw_slot_count(key, part):
    key_load, key_heavy, key_drop = jax.random.split(jax.random.fold_in(key, 7), 3)
    load = jax.random.randint(key_load, (OWNERS,), CAP // 8 + 1, CAP + 1)
    heavy = jax.random.randint(key_heavy, (), 0, OWNERS)
    is_heavy = jnp.arange(OWNERS) == heavy
    load = jnp.where(is_heavy, CAP, load)
    sources = jnp.arange(OWNERS)[:, None]
    members = jnp.arange(N_BLK)[None, :]
    owner_id = sources // N_BLK * N_BLK + members
    drop = jax.random.randint(key_drop, (OWNERS, N_BLK), 0, CAP // 4 + 1)
    counts = jnp.maximum(load[owner_id] - drop, 1)
    counts = jnp.where(is_heavy[owner_id], CAP, counts)
    return counts.reshape(OWNERS * N_BLK).astype(jnp.int32)


def draw_source_cell(key, part):
    key_row, key_col = jax.random.split(jax.random.fold_in(key, 11), 2)
    rows = jnp.arange(OWNERS * N_BLK)[:, None]
    sender = rows // N_BLK
    member = rows % N_BLK
    offset = (member - sender % N_BLK) % N_BLK
    cell_row = jax.random.randint(key_row, (OWNERS * N_BLK, CAP), 0, SX)
    spread = jax.random.randint(key_col, (OWNERS * N_BLK, CAP), 0, max(SY // 2, 1))
    cell_col = (offset * SY // N_BLK + spread) % SY
    return (cell_row * SY + cell_col).astype(jnp.int32)


def draw_target_cell(key, part):
    key_spot = jax.random.fold_in(key, 13)
    rows = jnp.arange(OWNERS * N_BLK)[:, None]
    owner = rows // N_BLK
    member = rows % N_BLK
    offset = (member - owner % N_BLK) % N_BLK
    spread = jax.random.randint(key_spot, (OWNERS * N_BLK, CAP), 0, max(TC // 2, 1))
    return ((offset * TC // N_BLK + spread) % TC).astype(jnp.int32)


def steps_of(stream_key, extent, cuts, smallest, high):
    def one(dim, parts):
        draws = jax.random.uniform(jax.random.fold_in(jax.random.fold_in(stream_key, 6), dim), (parts,), jnp.float32, smallest / len(cuts), high / len(cuts))
        return jnp.repeat(jnp.exp(draws), extent[dim] // parts).reshape((-1,) + (1,) * (len(extent) - dim - 1))

    factor_of = one(*cuts[0])
    for cut in cuts[1:]:
        factor_of = factor_of * one(*cut)
    return factor_of


def gaussian(key, extent, deviation, reach, shards=(), kind=jnp.bfloat16):
    values = deviation * jax.random.normal(key, extent, jnp.float32)
    if shards:
        values = values * steps_of(key, extent, shards, -0.22, 0.18)
    return jnp.clip(values, -reach, reach).astype(kind)


def setup_inputs(seed: int = 0) -> dict:
    splits = jax.random.split(jax.random.key(seed), 8)
    source_flux = gaussian(splits[0], (F, NSX, NSY), 1.0, 6.0, ((1, 8), (2, 16)))
    gauss_weight = jnp.clip(jnp.exp(math.log(0.2) - 2.3025851 * jax.random.uniform(splits[1], (Q, OWNERS * N_BLK, CAP), jnp.float32) ** steps_of(splits[1], (Q, OWNERS * N_BLK, CAP), ((1, 128),), -0.2, 0.2)), 0.02, 0.2)
    gauss_offset = jnp.clip(jax.random.uniform(splits[2], (2, Q, OWNERS * N_BLK, CAP), jnp.float32, -0.5, 0.5) * steps_of(splits[2], (2, Q, OWNERS * N_BLK, CAP), ((2, 128),), -0.4, 0.0), -0.5, 0.5)
    slot_count = draw_slot_count(jax.random.fold_in(splits[7], 71), 0)
    source_cell = draw_source_cell(jax.random.fold_in(splits[7], 71), 0)
    target_cell = draw_target_cell(jax.random.fold_in(splits[7], 71), 0)
    target_area = jnp.clip(jnp.exp(math.log(1.0) - 1.3862944 * jax.random.uniform(splits[6], (OWNERS * TC,), jnp.float32) ** steps_of(splits[6], (OWNERS * TC,), ((0, 128),), -0.2, 0.2)), 0.25, 1.0)
    return {"source_flux": source_flux, "gauss_weight": gauss_weight, "gauss_offset": gauss_offset, "slot_count": slot_count, "source_cell": source_cell, "target_cell": target_cell, "target_area": target_area}


def rim_slice(block, along, offset, height, breadth):
    if along == 0:
        return block[:, 2 + offset:2 + offset + height, 2:2 + breadth]
    return block[:, 2:2 + height, 2 + offset:2 + offset + breadth]


def reconstruct(block, height, breadth):
    center = rim_slice(block, 0, 0, height, breadth)
    along_x = [rim_slice(block, 0, offset, height, breadth) for offset in (-2, -1, 1, 2)]
    along_y = [rim_slice(block, 1, offset, height, breadth) for offset in (-2, -1, 1, 2)]
    slope_x = (along_x[0] - 8.0 * along_x[1] + 8.0 * along_x[2] - along_x[3]) / 12.0
    curve_x = (-along_x[0] + 16.0 * along_x[1] - 30.0 * center + 16.0 * along_x[2] - along_x[3]) / 12.0
    slope_y = (along_y[0] - 8.0 * along_y[1] + 8.0 * along_y[2] - along_y[3]) / 12.0
    curve_y = (-along_y[0] + 16.0 * along_y[1] - 30.0 * center + 16.0 * along_y[2] - along_y[3]) / 12.0
    stacked = jnp.stack([center, slope_x, slope_y, curve_x, curve_y])
    return stacked.reshape(5, block.shape[0], height * breadth)


def reference(source_flux, gauss_weight, gauss_offset, slot_count, source_cell, target_cell, target_area):
    owners = N_PANEL * N_BLK
    wrapped = jnp.concatenate([source_flux[:, :, -2:], source_flux, source_flux[:, :, :2]], axis=2)
    padded = jnp.pad(wrapped, ((0, 0), (2, 2), (0, 0)))
    weight = gauss_weight.reshape(Q, owners, N_BLK, CAP)
    offset_x = gauss_offset[0].reshape(Q, owners, N_BLK, CAP)
    offset_y = gauss_offset[1].reshape(Q, owners, N_BLK, CAP)
    moments = jnp.stack([
        jnp.sum(weight, axis=0),
        jnp.sum(weight * offset_x, axis=0),
        jnp.sum(weight * offset_y, axis=0),
        0.5 * jnp.sum(weight * offset_x * offset_x, axis=0),
        0.5 * jnp.sum(weight * offset_y * offset_y, axis=0)])
    slots = jnp.arange(CAP).astype(jnp.int32)
    live_mask = (slots[None, None, :] < slot_count.reshape(owners, N_BLK)[:, :, None]).astype(jnp.float32)
    coefficient = moments * live_mask[None]
    cells = source_cell.reshape(owners, N_BLK, CAP)
    targets = target_cell.reshape(owners, N_BLK, CAP)
    band_rows = jnp.arange(N_BLK).astype(jnp.int32)

    def accumulate(summed, source):
        source = source.astype(jnp.int32)
        band = (source // N_BLK).astype(jnp.int32)
        column = (source % N_BLK).astype(jnp.int32)
        row_start = (band * SX).astype(jnp.int32)
        col_start = (column * SY).astype(jnp.int32)
        block = lax.dynamic_slice(padded, (jnp.int32(0), row_start, col_start), (F, SX + 4, SY + 4)).astype(jnp.float32)
        recon = reconstruct(block, SX, SY)
        picked = jnp.take(recon, cells[source].reshape(-1), axis=2).reshape(5, F, N_BLK, CAP)
        record_value = jnp.sum(picked * coefficient[:, source][:, None], axis=0)
        rounded = lax.optimization_barrier(record_value.astype(jnp.bfloat16)).astype(jnp.float32)
        dest_owner = (band * N_BLK + band_rows).astype(jnp.int32)
        dest_cells = targets[dest_owner, column, :]
        summed = summed.at[dest_owner[:, None], dest_cells].add(jnp.transpose(rounded, (1, 2, 0)))
        return summed, None

    start = jnp.zeros((owners, TC, F), jnp.float32)
    summed, unused = lax.scan(accumulate, start, jnp.arange(owners).astype(jnp.int32))
    result = summed / target_area.reshape(owners, TC)[:, :, None]
    return jnp.transpose(result, (2, 0, 1)).reshape(F, owners * TC).astype(jnp.bfloat16)
```

```python
import functools

import jax
import jax.numpy as jnp
from jax import lax
from jax.experimental import pallas as pl
from jax.experimental.pallas import tpu as pltpu
from jax.sharding import PartitionSpec as P

GROUP = 8
REACH = 2
LOW = 256
TERMS = 16


def record_body(window_ref, rim_ref, term_ref, out_ref, *, fields, height, breadth):
    groups = height // GROUP
    span = GROUP + 2 * REACH
    terms = term_ref[0]
    slots = terms.shape[1]
    scale = terms[0:1]
    row_taps = [terms[1 + i : 2 + i] for i in range(4)]
    col_taps = [terms[5 + i : 6 + i] for i in range(4)]
    row = terms[9:10].astype(jnp.int32)
    col = terms[10:11].astype(jnp.int32)
    shifts = (-2, -1, 1, 2)
    group = row // GROUP
    local = row - group * GROUP + REACH
    gap = lax.broadcasted_iota(jnp.int32, (breadth, slots), 0) - col
    here = jnp.where(gap == 0, 1.0, 0.0).astype(jnp.bfloat16)
    beside = jnp.zeros((breadth, slots), jnp.float32)
    for shift, tap in zip(shifts, col_taps):
        beside = jnp.where(gap == shift, tap, beside)
    beside = beside.astype(jnp.bfloat16)
    pieces = []
    for j in range(span):
        centre = jnp.where(local == j, 1.0, 0.0)
        weight = centre
        for shift, tap in zip(shifts, row_taps):
            weight = jnp.where(local + shift == j, tap, weight)
        pieces.append(
            here * weight.astype(jnp.bfloat16) + beside * centre.astype(jnp.bfloat16)
        )
    table = jnp.concatenate(pieces, axis=0)
    product = jnp.dot(window_ref[...], table, preferred_element_type=jnp.float32)
    same_row = jnp.where(
        lax.broadcasted_iota(jnp.int32, (height, slots), 0) == row, 1.0, 0.0
    ).astype(jnp.bfloat16)
    rim_pieces = []
    for place in (-2, -1, breadth, breadth + 1):
        weight = jnp.zeros((1, slots), jnp.float32)
        for shift, tap in zip(shifts, col_taps):
            weight = jnp.where(col + shift == place, tap, weight)
        rim_pieces.append(same_row * weight.astype(jnp.bfloat16))
    total = jnp.dot(
        rim_ref[...], jnp.concatenate(rim_pieces, axis=0), preferred_element_type=jnp.float32
    )
    for g in range(groups):
        total = total + jnp.where(group == g, product[g * fields : (g + 1) * fields], 0.0)
    out_ref[0] = (total * scale).astype(jnp.bfloat16)


def deposit_body(record_ref, target_ref, area_ref, out_ref, total_ref, *, fields, cells):
    step = pl.program_id(0)
    highs = cells // LOW
    target = target_ref[0]
    capacity = target.shape[1]
    high = target // LOW
    low = target - high * LOW
    values = record_ref[0].astype(jnp.float32)
    spread = jnp.concatenate(
        [jnp.where(high == h, values, 0.0) for h in range(highs)], axis=0
    ).astype(jnp.bfloat16)
    place = jnp.where(
        lax.broadcasted_iota(jnp.int32, (LOW, capacity), 0) == low, 1.0, 0.0
    ).astype(jnp.bfloat16)
    part = lax.dot_general(
        spread, place, (((1,), (1,)), ((), ())), preferred_element_type=jnp.float32
    )

    @pl.when(step == 0)
    def first():
        total_ref[...] = part

    @pl.when(step > 0)
    def later():
        total_ref[...] = total_ref[...] + part

    @pl.when(step == pl.num_programs(0) - 1)
    def finish():
        for h in range(highs):
            area = area_ref[:, h * LOW : (h + 1) * LOW]
            out_ref[:, h * LOW : (h + 1) * LOW] = (
                total_ref[h * fields : (h + 1) * fields, :] / area
            ).astype(jnp.bfloat16)


def neighbours(first, last, axis, wrap):
    size = lax.axis_size(axis)
    up = [(i, (i + 1) % size) for i in range(size if wrap else size - 1)]
    down = [(j, i) for i, j in up]
    return (lax.ppermute(last, axis, up), lax.ppermute(first, axis, down))


def on_device(
    source_flux, gauss_weight, gauss_offset, slot_count, source_cell, target_cell, target_area
):
    fields, height, breadth = source_flux.shape
    members = lax.axis_size("blk")
    capacity = source_cell.shape[1]
    cells = target_area.shape[0]
    groups = height // GROUP
    span = GROUP + 2 * REACH
    above, below = neighbours(
        source_flux[:, :REACH], source_flux[:, height - REACH :], "panel", False
    )
    flat = lambda part: jnp.swapaxes(part, 1, 2).reshape(fields, REACH * height)
    before, after = neighbours(
        flat(source_flux[:, :, :REACH]), flat(source_flux[:, :, breadth - REACH :]), "blk", True
    )
    rim = jnp.concatenate([before, after], axis=1)
    tall = jnp.concatenate([above, source_flux, below], axis=1)
    window = jnp.stack([tall[:, g * GROUP : g * GROUP + span] for g in range(groups)]).reshape(
        groups * fields, span * breadth
    )
    offset_x = gauss_offset[0]
    offset_y = gauss_offset[1]
    slots = lax.broadcasted_iota(jnp.int32, (members, capacity), 1)
    live = (slots < slot_count[:, None]).astype(jnp.float32)
    area = jnp.sum(gauss_weight, axis=0)
    first_x = jnp.sum(gauss_weight * offset_x, axis=0)
    first_y = jnp.sum(gauss_weight * offset_y, axis=0)
    second_x = 0.5 * jnp.sum(gauss_weight * offset_x * offset_x, axis=0)
    second_y = 0.5 * jnp.sum(gauss_weight * offset_y * offset_y, axis=0)
    centre = area - 2.5 * (second_x + second_y)
    inverse = 1.0 / (12.0 * centre)
    taps = []
    for one, two in ((first_x, second_x), (first_y, second_y)):
        taps += [
            (one - two) * inverse,
            (16.0 * two - 8.0 * one) * inverse,
            (16.0 * two + 8.0 * one) * inverse,
            (-one - two) * inverse,
        ]
    row = source_cell // breadth
    col = source_cell - row * breadth
    terms = [centre * live] + taps + [row.astype(jnp.float32), col.astype(jnp.float32)]
    terms += [jnp.zeros_like(area)] * (TERMS - len(terms))
    terms = jnp.stack(terms, axis=1)
    records = pl.pallas_call(
        functools.partial(record_body, fields=fields, height=height, breadth=breadth),
        grid=(members,),
        in_specs=[
            pl.BlockSpec((groups * fields, span * breadth), lambda i: (0, 0)),
            pl.BlockSpec((fields, 2 * REACH * height), lambda i: (0, 0)),
            pl.BlockSpec((1, TERMS, capacity), lambda i: (i, 0, 0)),
        ],
        out_specs=pl.BlockSpec((1, fields, capacity), lambda i: (i, 0, 0)),
        out_shape=jax.ShapeDtypeStruct((members, fields, capacity), jnp.bfloat16),
        name="records",
    )(window, rim, terms)
    arrived = lax.all_to_all(records, "blk", split_axis=0, concat_axis=0, tiled=True)
    return pl.pallas_call(
        functools.partial(deposit_body, fields=fields, cells=cells),
        grid=(members,),
        in_specs=[
            pl.BlockSpec((1, fields, capacity), lambda i: (i, 0, 0)),
            pl.BlockSpec((1, 1, capacity), lambda i: (i, 0, 0)),
            pl.BlockSpec((1, cells), lambda i: (0, 0)),
        ],
        out_specs=pl.BlockSpec((fields, cells), lambda i: (0, 0)),
        out_shape=jax.ShapeDtypeStruct((fields, cells), jnp.bfloat16),
        scratch_shapes=[pltpu.VMEM((cells // LOW * fields, LOW), jnp.float32)],
        name="deposit",
    )(arrived, target_cell.reshape(members, 1, capacity), target_area.reshape(1, cells))


def solution(mesh):
    placed = (
        P(None, "panel", "blk"),
        P(None, ("panel", "blk"), None),
        P(None, None, ("panel", "blk"), None),
        P(("panel", "blk")),
        P(("panel", "blk"), None),
        P(("panel", "blk"), None),
        P(("panel", "blk")),
    )
    return jax.shard_map(
        on_device, mesh=mesh, in_specs=placed, out_specs=P(None, ("panel", "blk")), check_vma=False
    )
```

```python
import functools

import jax
import jax.numpy as jnp
from jax import lax
from jax.experimental import pallas as pl
from jax.experimental.pallas import tpu as pltpu
from jax.sharding import PartitionSpec as P

GROUP = 8
REACH = 2
LOW = 256
TERMS = 16
BATCH = 8


def record_body(
    count_ref, window_ref, rim_ref, term_ref, out_ref, *, fields, height, breadth, start
):
    groups = height // GROUP
    span = GROUP + 2 * REACH
    alive = count_ref[pl.program_id(0)] > start

    @pl.when(alive)
    def compute():
        terms = term_ref[0]
        slots = terms.shape[1]
        scale = terms[0:1]
        row_taps = [terms[1 + i : 2 + i] for i in range(4)]
        col_taps = [terms[5 + i : 6 + i] for i in range(4)]
        row = terms[9:10].astype(jnp.int32)
        col = terms[10:11].astype(jnp.int32)
        shifts = (-2, -1, 1, 2)
        group = row // GROUP
        local = row - group * GROUP + REACH
        gap = lax.broadcasted_iota(jnp.int32, (breadth, slots), 0) - col
        here = jnp.where(gap == 0, 1.0, 0.0).astype(jnp.bfloat16)
        beside = jnp.zeros((breadth, slots), jnp.float32)
        for shift, tap in zip(shifts, col_taps):
            beside = jnp.where(gap == shift, tap, beside)
        beside = beside.astype(jnp.bfloat16)
        pieces = []
        for j in range(span):
            centre = jnp.where(local == j, 1.0, 0.0)
            weight = centre
            for shift, tap in zip(shifts, row_taps):
                weight = jnp.where(local + shift == j, tap, weight)
            pieces.append(
                here * weight.astype(jnp.bfloat16) + beside * centre.astype(jnp.bfloat16)
            )
        table = jnp.concatenate(pieces, axis=0)
        product = jnp.dot(window_ref[...], table, preferred_element_type=jnp.float32)
        same_row = jnp.where(
            lax.broadcasted_iota(jnp.int32, (height, slots), 0) == row, 1.0, 0.0
        ).astype(jnp.bfloat16)
        rim_pieces = []
        for place in (-2, -1, breadth, breadth + 1):
            weight = jnp.zeros((1, slots), jnp.float32)
            for shift, tap in zip(shifts, col_taps):
                weight = jnp.where(col + shift == place, tap, weight)
            rim_pieces.append(same_row * weight.astype(jnp.bfloat16))
        total = jnp.dot(
            rim_ref[...], jnp.concatenate(rim_pieces, axis=0), preferred_element_type=jnp.float32
        )
        for g in range(groups):
            total = total + jnp.where(group == g, product[g * fields : (g + 1) * fields], 0.0)
        out_ref[0] = (total * scale).astype(jnp.bfloat16)

    @pl.when(jnp.logical_not(alive))
    def clear():
        out_ref[...] = jnp.zeros(out_ref.shape, out_ref.dtype)


def deposit_part(record_ref, target_ref, *, highs, padded):
    batch, fields, _ = record_ref.shape
    target = jnp.concatenate([target_ref[b] for b in range(batch)], axis=1)
    values = jnp.concatenate([record_ref[b] for b in range(batch)], axis=1).astype(jnp.float32)
    slots = target.shape[1]
    values = jnp.concatenate(
        [values, jnp.zeros((padded - fields, slots), jnp.float32)], axis=0
    ).astype(jnp.bfloat16)
    high = target // LOW
    low = target - high * LOW
    spread = jnp.concatenate(
        [values * jnp.where(high == h, 1.0, 0.0).astype(jnp.bfloat16) for h in range(highs)],
        axis=0,
    )
    place = jnp.where(
        lax.broadcasted_iota(jnp.int32, (LOW, slots), 0) == low, 1.0, 0.0
    ).astype(jnp.bfloat16)
    return lax.dot_general(
        spread, place, (((1,), (1,)), ((), ())), preferred_element_type=jnp.float32
    )


def deposit_first_body(record_ref, target_ref, total_ref, *, highs, padded):
    part = deposit_part(record_ref, target_ref, highs=highs, padded=padded)

    @pl.when(pl.program_id(0) == 0)
    def first():
        total_ref[...] = part

    @pl.when(pl.program_id(0) > 0)
    def later():
        total_ref[...] = total_ref[...] + part


def deposit_last_body(
    record_ref, target_ref, before_ref, area_ref, out_ref, total_ref, *, highs, padded
):
    step = pl.program_id(0)
    fields = out_ref.shape[0]
    part = deposit_part(record_ref, target_ref, highs=highs, padded=padded)

    @pl.when(step == 0)
    def first():
        total_ref[...] = before_ref[...] + part

    @pl.when(step > 0)
    def later():
        total_ref[...] = total_ref[...] + part

    @pl.when(step == pl.num_programs(0) - 1)
    def finish():
        for h in range(highs):
            area = area_ref[:, h * LOW : (h + 1) * LOW]
            out_ref[:, h * LOW : (h + 1) * LOW] = (
                total_ref[h * padded : h * padded + fields, :] / area
            ).astype(jnp.bfloat16)


def neighbours(first, last, axis, wrap):
    size = lax.axis_size(axis)
    up = [(i, (i + 1) % size) for i in range(size if wrap else size - 1)]
    down = [(j, i) for i, j in up]
    return (lax.ppermute(last, axis, up), lax.ppermute(first, axis, down))


def on_device(
    source_flux, gauss_weight, gauss_offset, slot_count, source_cell, target_cell, target_area
):
    fields, height, breadth = source_flux.shape
    members = lax.axis_size("blk")
    capacity = source_cell.shape[1]
    cells = target_area.shape[0]
    groups = height // GROUP
    span = GROUP + 2 * REACH
    above, below = neighbours(
        source_flux[:, :REACH], source_flux[:, height - REACH :], "panel", False
    )
    flat = lambda part: jnp.swapaxes(part, 1, 2).reshape(fields, REACH * height)
    before, after = neighbours(
        flat(source_flux[:, :, :REACH]), flat(source_flux[:, :, breadth - REACH :]), "blk", True
    )
    rim = jnp.concatenate([before, after], axis=1)
    tall = jnp.concatenate([above, source_flux, below], axis=1)
    window = jnp.stack([tall[:, g * GROUP : g * GROUP + span] for g in range(groups)]).reshape(
        groups * fields, span * breadth
    )
    offset_x = gauss_offset[0]
    offset_y = gauss_offset[1]
    slots = lax.broadcasted_iota(jnp.int32, (members, capacity), 1)
    live = (slots < slot_count[:, None]).astype(jnp.float32)
    area = jnp.sum(gauss_weight, axis=0)
    first_x = jnp.sum(gauss_weight * offset_x, axis=0)
    first_y = jnp.sum(gauss_weight * offset_y, axis=0)
    second_x = 0.5 * jnp.sum(gauss_weight * offset_x * offset_x, axis=0)
    second_y = 0.5 * jnp.sum(gauss_weight * offset_y * offset_y, axis=0)
    centre = area - 2.5 * (second_x + second_y)
    inverse = 1.0 / (12.0 * centre)
    taps = []
    for one, two in ((first_x, second_x), (first_y, second_y)):
        taps += [
            (one - two) * inverse,
            (16.0 * two - 8.0 * one) * inverse,
            (16.0 * two + 8.0 * one) * inverse,
            (-one - two) * inverse,
        ]
    row = source_cell // breadth
    col = source_cell - row * breadth
    terms = [centre * live] + taps + [row.astype(jnp.float32), col.astype(jnp.float32)]
    terms += [jnp.zeros_like(area)] * (TERMS - len(terms))
    terms = jnp.stack(terms, axis=1)
    half = capacity // 2
    arrived = []
    for part in range(2):
        records = pl.pallas_call(
            functools.partial(
                record_body, fields=fields, height=height, breadth=breadth, start=part * half
            ),
            grid_spec=pltpu.PrefetchScalarGridSpec(
                num_scalar_prefetch=1,
                grid=(members,),
                in_specs=[
                    pl.BlockSpec((groups * fields, span * breadth), lambda i, n: (0, 0)),
                    pl.BlockSpec((fields, 2 * REACH * height), lambda i, n: (0, 0)),
                    pl.BlockSpec((1, TERMS, half), lambda i, n, part=part: (i, 0, part)),
                ],
                out_specs=pl.BlockSpec((1, fields, half), lambda i, n: (i, 0, 0)),
            ),
            out_shape=jax.ShapeDtypeStruct((members, fields, half), jnp.bfloat16),
            name=f"records_{part}",
        )(slot_count, window, rim, terms)
        arrived.append(lax.all_to_all(records, "blk", split_axis=0, concat_axis=0, tiled=True))
    highs = cells // LOW
    padded = -(-fields // 16) * 16
    targets = target_cell.reshape(members, 1, capacity)
    record_spec = pl.BlockSpec((BATCH, fields, half), lambda i: (i, 0, 0))
    total_spec = pl.BlockSpec((highs * padded, LOW), lambda i: (0, 0))
    before = pl.pallas_call(
        functools.partial(deposit_first_body, highs=highs, padded=padded),
        grid=(members // BATCH,),
        in_specs=[record_spec, pl.BlockSpec((BATCH, 1, half), lambda i: (i, 0, 0))],
        out_specs=total_spec,
        out_shape=jax.ShapeDtypeStruct((highs * padded, LOW), jnp.float32),
        name="deposit_0",
    )(arrived[0], targets)
    return pl.pallas_call(
        functools.partial(deposit_last_body, highs=highs, padded=padded),
        grid=(members // BATCH,),
        in_specs=[
            record_spec,
            pl.BlockSpec((BATCH, 1, half), lambda i: (i, 0, 1)),
            total_spec,
            pl.BlockSpec((1, cells), lambda i: (0, 0)),
        ],
        out_specs=pl.BlockSpec((fields, cells), lambda i: (0, 0)),
        out_shape=jax.ShapeDtypeStruct((fields, cells), jnp.bfloat16),
        scratch_shapes=[pltpu.VMEM((highs * padded, LOW), jnp.float32)],
        name="deposit_1",
    )(arrived[1], targets, before, target_area.reshape(1, cells))


def solution(mesh):
    placed = (
        P(None, "panel", "blk"),
        P(None, ("panel", "blk"), None),
        P(None, None, ("panel", "blk"), None),
        P(("panel", "blk")),
        P(("panel", "blk"), None),
        P(("panel", "blk"), None),
        P(("panel", "blk")),
    )
    return jax.shard_map(
        on_device, mesh=mesh, in_specs=placed, out_specs=P(None, ("panel", "blk")), check_vma=False
    )
```

```python
import functools

import jax
import jax.numpy as jnp
from jax import lax
from jax.experimental import pallas as pl
from jax.experimental.pallas import tpu as pltpu
from jax.sharding import PartitionSpec as P

GROUP = 8
REACH = 2
LOW = 256
TERMS = 16
BATCH = 8
OWNERS = 4


def slot_records(terms, window_ref, rim, *, fields, height, breadth):
    groups = height // GROUP
    span = GROUP + 2 * REACH
    slots = terms.shape[1]
    scale = terms[0:1]
    row_taps = [terms[1 + i : 2 + i] for i in range(4)]
    col_taps = [terms[5 + i : 6 + i] for i in range(4)]
    row = terms[9:10].astype(jnp.int32)
    col = terms[10:11].astype(jnp.int32)
    shifts = (-2, -1, 1, 2)
    group = row // GROUP
    local = row - group * GROUP + REACH
    gap = lax.broadcasted_iota(jnp.int32, (breadth, slots), 0) - col
    here = jnp.where(gap == 0, 1.0, 0.0).astype(jnp.bfloat16)
    beside = jnp.zeros((breadth, slots), jnp.float32)
    for shift, tap in zip(shifts, col_taps):
        beside = jnp.where(gap == shift, tap, beside)
    beside = beside.astype(jnp.bfloat16)
    pieces = []
    for j in range(span):
        centre = jnp.where(local == j, 1.0, 0.0)
        weight = centre
        for shift, tap in zip(shifts, row_taps):
            weight = jnp.where(local + shift == j, tap, weight)
        pieces.append(here * weight.astype(jnp.bfloat16) + beside * centre.astype(jnp.bfloat16))
    table = jnp.concatenate(pieces, axis=0)
    product = jnp.dot(window_ref[...], table, preferred_element_type=jnp.float32)
    same_row = jnp.where(
        lax.broadcasted_iota(jnp.int32, (height, slots), 0) == row, 1.0, 0.0
    ).astype(jnp.bfloat16)
    rim_pieces = []
    for place in (-2, -1, breadth, breadth + 1):
        weight = jnp.zeros((1, slots), jnp.float32)
        for shift, tap in zip(shifts, col_taps):
            weight = jnp.where(col + shift == place, tap, weight)
        rim_pieces.append(same_row * weight.astype(jnp.bfloat16))
    total = jnp.dot(rim, jnp.concatenate(rim_pieces, axis=0), preferred_element_type=jnp.float32)
    for g in range(groups):
        total = total + jnp.where(group == g, product[g * fields : (g + 1) * fields], 0.0)
    return (total * scale).astype(jnp.bfloat16)


def record_body(
    count_ref,
    window_ref,
    above_ref,
    below_ref,
    before_ref,
    after_ref,
    term_ref,
    out_ref,
    full_ref,
    *,
    fields,
    height,
    breadth,
    start,
):
    step = pl.program_id(0)
    batch, _, slots = term_ref.shape
    edge = REACH * breadth

    @pl.when(step == 0)
    def fill():
        full_ref[...] = window_ref[...]
        full_ref[:fields, :edge] = above_ref[...]
        full_ref[-fields:, -edge:] = below_ref[...]

    rim = jnp.concatenate([before_ref[...], after_ref[...]], axis=1)
    make = functools.partial(slot_records, fields=fields, height=height, breadth=breadth)
    if start == 0:
        terms = jnp.concatenate([term_ref[b] for b in range(batch)], axis=1)
        made = make(terms, full_ref, rim)
        for b in range(batch):
            out_ref[b] = made[:, b * slots : (b + 1) * slots]
    else:
        for b in range(batch):
            alive = count_ref[step * batch + b] > start

            @pl.when(alive)
            def compute():
                out_ref[b] = make(term_ref[b], full_ref, rim)

            @pl.when(jnp.logical_not(alive))
            def clear():
                out_ref[b] = jnp.zeros((fields, slots), out_ref.dtype)


def deposit_part(record_ref, target_ref, *, highs, padded):
    batch, fields, _ = record_ref.shape
    target = jnp.concatenate([target_ref[b] for b in range(batch)], axis=1)
    values = jnp.concatenate([record_ref[b] for b in range(batch)], axis=1).astype(jnp.float32)
    slots = target.shape[1]
    values = jnp.concatenate(
        [values, jnp.zeros((padded - fields, slots), jnp.float32)], axis=0
    ).astype(jnp.bfloat16)
    high = target // LOW
    low = target - high * LOW
    spread = jnp.concatenate(
        [values * jnp.where(high == h, 1.0, 0.0).astype(jnp.bfloat16) for h in range(highs)],
        axis=0,
    )
    place = jnp.where(
        lax.broadcasted_iota(jnp.int32, (LOW, slots), 0) == low, 1.0, 0.0
    ).astype(jnp.bfloat16)
    return lax.dot_general(
        spread, place, (((1,), (1,)), ((), ())), preferred_element_type=jnp.float32
    )


def deposit_first_body(record_ref, target_ref, total_ref, *, highs, padded):
    part = deposit_part(record_ref, target_ref, highs=highs, padded=padded)

    @pl.when(pl.program_id(0) == 0)
    def first():
        total_ref[...] = part

    @pl.when(pl.program_id(0) > 0)
    def later():
        total_ref[...] = total_ref[...] + part


def deposit_last_body(
    record_ref, target_ref, before_ref, area_ref, out_ref, total_ref, *, highs, padded
):
    step = pl.program_id(0)
    fields = out_ref.shape[0]
    part = deposit_part(record_ref, target_ref, highs=highs, padded=padded)

    @pl.when(step == 0)
    def first():
        total_ref[...] = before_ref[...] + part

    @pl.when(step > 0)
    def later():
        total_ref[...] = total_ref[...] + part

    @pl.when(step == pl.num_programs(0) - 1)
    def finish():
        for h in range(highs):
            area = area_ref[:, h * LOW : (h + 1) * LOW]
            out_ref[:, h * LOW : (h + 1) * LOW] = (
                total_ref[h * padded : h * padded + fields, :] / area
            ).astype(jnp.bfloat16)


def neighbours(first, last, axis, wrap):
    size = lax.axis_size(axis)
    up = [(i, (i + 1) % size) for i in range(size if wrap else size - 1)]
    down = [(j, i) for i, j in up]
    return (lax.ppermute(last, axis, up), lax.ppermute(first, axis, down))


def on_device(
    source_flux, gauss_weight, gauss_offset, slot_count, source_cell, target_cell, target_area
):
    fields, height, breadth = source_flux.shape
    members = lax.axis_size("blk")
    capacity = source_cell.shape[1]
    cells = target_area.shape[0]
    groups = height // GROUP
    span = GROUP + 2 * REACH
    flat_rows = lambda part: part.reshape(fields, REACH * breadth)
    flat_cols = lambda part: jnp.swapaxes(part, 1, 2).reshape(fields, REACH * height)
    above, below = neighbours(
        flat_rows(source_flux[:, :REACH]),
        flat_rows(source_flux[:, height - REACH :]),
        "panel",
        False,
    )
    before, after = neighbours(
        flat_cols(source_flux[:, :, :REACH]),
        flat_cols(source_flux[:, :, breadth - REACH :]),
        "blk",
        True,
    )
    tall = jnp.pad(source_flux, ((0, 0), (REACH, REACH), (0, 0)))
    window = jnp.stack([tall[:, g * GROUP : g * GROUP + span] for g in range(groups)]).reshape(
        groups * fields, span * breadth
    )
    offset_x = gauss_offset[0]
    offset_y = gauss_offset[1]
    slots = lax.broadcasted_iota(jnp.int32, (members, capacity), 1)
    live = (slots < slot_count[:, None]).astype(jnp.float32)
    area = jnp.sum(gauss_weight, axis=0)
    first_x = jnp.sum(gauss_weight * offset_x, axis=0)
    first_y = jnp.sum(gauss_weight * offset_y, axis=0)
    second_x = 0.5 * jnp.sum(gauss_weight * offset_x * offset_x, axis=0)
    second_y = 0.5 * jnp.sum(gauss_weight * offset_y * offset_y, axis=0)
    centre = area - 2.5 * (second_x + second_y)
    inverse = 1.0 / (12.0 * centre)
    taps = []
    for one, two in ((first_x, second_x), (first_y, second_y)):
        taps += [
            (one - two) * inverse,
            (16.0 * two - 8.0 * one) * inverse,
            (16.0 * two + 8.0 * one) * inverse,
            (-one - two) * inverse,
        ]
    row = source_cell // breadth
    col = source_cell - row * breadth
    terms = [centre * live] + taps + [row.astype(jnp.float32), col.astype(jnp.float32)]
    terms += [jnp.zeros_like(area)] * (TERMS - len(terms))
    terms = jnp.stack(terms, axis=1)
    half = capacity // 2
    arrived = []
    for part in range(2):
        records = pl.pallas_call(
            functools.partial(
                record_body, fields=fields, height=height, breadth=breadth, start=part * half
            ),
            grid_spec=pltpu.PrefetchScalarGridSpec(
                num_scalar_prefetch=1,
                grid=(members // OWNERS,),
                in_specs=[
                    pl.BlockSpec((groups * fields, span * breadth), lambda i, n: (0, 0)),
                    pl.BlockSpec((fields, REACH * breadth), lambda i, n: (0, 0)),
                    pl.BlockSpec((fields, REACH * breadth), lambda i, n: (0, 0)),
                    pl.BlockSpec((fields, REACH * height), lambda i, n: (0, 0)),
                    pl.BlockSpec((fields, REACH * height), lambda i, n: (0, 0)),
                    pl.BlockSpec((OWNERS, TERMS, half), lambda i, n, part=part: (i, 0, part)),
                ],
                out_specs=pl.BlockSpec((OWNERS, fields, half), lambda i, n: (i, 0, 0)),
                scratch_shapes=[
                    pltpu.VMEM((groups * fields, span * breadth), jnp.bfloat16)
                ],
            ),
            out_shape=jax.ShapeDtypeStruct((members, fields, half), jnp.bfloat16),
            name=f"records_{part}",
        )(slot_count, window, above, below, before, after, terms)
        arrived.append(lax.all_to_all(records, "blk", split_axis=0, concat_axis=0, tiled=True))
    highs = cells // LOW
    padded = -(-fields // 16) * 16
    targets = target_cell.reshape(members, 1, capacity)
    record_spec = pl.BlockSpec((BATCH, fields, half), lambda i: (i, 0, 0))
    total_spec = pl.BlockSpec((highs * padded, LOW), lambda i: (0, 0))
    before = pl.pallas_call(
        functools.partial(deposit_first_body, highs=highs, padded=padded),
        grid=(members // BATCH,),
        in_specs=[record_spec, pl.BlockSpec((BATCH, 1, half), lambda i: (i, 0, 0))],
        out_specs=total_spec,
        out_shape=jax.ShapeDtypeStruct((highs * padded, LOW), jnp.float32),
        name="deposit_0",
    )(arrived[0], targets)
    return pl.pallas_call(
        functools.partial(deposit_last_body, highs=highs, padded=padded),
        grid=(members // BATCH,),
        in_specs=[
            record_spec,
            pl.BlockSpec((BATCH, 1, half), lambda i: (i, 0, 1)),
            total_spec,
            pl.BlockSpec((1, cells), lambda i: (0, 0)),
        ],
        out_specs=pl.BlockSpec((fields, cells), lambda i: (0, 0)),
        out_shape=jax.ShapeDtypeStruct((fields, cells), jnp.bfloat16),
        scratch_shapes=[pltpu.VMEM((highs * padded, LOW), jnp.float32)],
        name="deposit_1",
    )(arrived[1], targets, before, target_area.reshape(1, cells))


def solution(mesh):
    placed = (
        P(None, "panel", "blk"),
        P(None, ("panel", "blk"), None),
        P(None, None, ("panel", "blk"), None),
        P(("panel", "blk")),
        P(("panel", "blk"), None),
        P(("panel", "blk"), None),
        P(("panel", "blk")),
    )
    return jax.shard_map(
        on_device, mesh=mesh, in_specs=placed, out_specs=P(None, ("panel", "blk")), check_vma=False
    )
```

```python
import functools

import jax
import jax.numpy as jnp
import numpy as np
from jax import lax
from jax.experimental import pallas as pl
from jax.experimental.pallas import tpu as pltpu
from jax.sharding import PartitionSpec as P

GROUP = 8
REACH = 2
LOW = 256
TERMS = 11
BATCH = 8
OWNERS = 4


def slot_records(terms, window_ref, rim, *, fields, height, breadth):
    groups = height // GROUP
    span = GROUP + 2 * REACH
    slots = terms[0].shape[1]
    scale = terms[0]
    row_taps = terms[1:5]
    col_taps = terms[5:9]
    row = terms[9].astype(jnp.int32)
    col = terms[10].astype(jnp.int32)
    shifts = (-2, -1, 1, 2)
    group = row // GROUP
    local = row - group * GROUP + REACH
    gap = lax.broadcasted_iota(jnp.int32, (breadth, slots), 0) - col
    here = jnp.where(gap == 0, 1.0, 0.0).astype(jnp.bfloat16)
    beside = jnp.zeros((breadth, slots), jnp.float32)
    for shift, tap in zip(shifts, col_taps):
        beside = jnp.where(gap == shift, tap, beside)
    beside = beside.astype(jnp.bfloat16)
    pieces = []
    for j in range(span):
        centre = jnp.where(local == j, 1.0, 0.0)
        weight = centre
        for shift, tap in zip(shifts, row_taps):
            weight = jnp.where(local + shift == j, tap, weight)
        pieces.append(here * weight.astype(jnp.bfloat16) + beside * centre.astype(jnp.bfloat16))
    table = jnp.concatenate(pieces, axis=0)
    product = jnp.dot(window_ref[...], table, preferred_element_type=jnp.float32)
    same_row = jnp.where(
        lax.broadcasted_iota(jnp.int32, (height, slots), 0) == row, 1.0, 0.0
    ).astype(jnp.bfloat16)
    rim_pieces = []
    for place in (-2, -1, breadth, breadth + 1):
        weight = jnp.zeros((1, slots), jnp.float32)
        for shift, tap in zip(shifts, col_taps):
            weight = jnp.where(col + shift == place, tap, weight)
        rim_pieces.append(same_row * weight.astype(jnp.bfloat16))
    total = jnp.dot(rim, jnp.concatenate(rim_pieces, axis=0), preferred_element_type=jnp.float32)
    for g in range(groups):
        total = total + jnp.where(group == g, product[g * fields : (g + 1) * fields], 0.0)
    return (total * scale).astype(jnp.bfloat16)


def slot_terms(weight, offset, cell, count, *, start, breadth):
    offset_x = offset[0]
    offset_y = offset[1]
    slots = lax.broadcasted_iota(jnp.int32, cell.shape, 1) + start
    live = jnp.where(slots < count, 1.0, 0.0)
    area = jnp.sum(weight, axis=0)
    first_x = jnp.sum(weight * offset_x, axis=0)
    first_y = jnp.sum(weight * offset_y, axis=0)
    second_x = 0.5 * jnp.sum(weight * offset_x * offset_x, axis=0)
    second_y = 0.5 * jnp.sum(weight * offset_y * offset_y, axis=0)
    centre = area - 2.5 * (second_x + second_y)
    inverse = 1.0 / (12.0 * centre)
    terms = [centre * live]
    for one, two in ((first_x, second_x), (first_y, second_y)):
        terms += [
            (one - two) * inverse,
            (16.0 * two - 8.0 * one) * inverse,
            (16.0 * two + 8.0 * one) * inverse,
            (-one - two) * inverse,
        ]
    row = cell // breadth
    col = cell - row * breadth
    return terms + [row.astype(jnp.float32), col.astype(jnp.float32)]


def record_body(
    count_ref,
    rows_ref,
    above_ref,
    below_ref,
    before_ref,
    after_ref,
    weight_ref,
    offset_ref,
    cell_ref,
    counts_ref,
    out_ref,
    full_ref,
    rim_ref,
    term_ref,
    *,
    start,
):
    step = pl.program_id(0)
    height, fields, breadth = rows_ref.shape
    batch, _, slots = out_ref.shape

    @pl.when(step == 0)
    def fill():
        for g in range(height // GROUP):
            for j in range(GROUP + 2 * REACH):
                r = g * GROUP + j - REACH
                if r < 0:
                    part = above_ref[r + REACH]
                elif r >= height:
                    part = below_ref[r - height]
                else:
                    part = rows_ref[r]
                full_ref[g * fields : (g + 1) * fields, j * breadth : (j + 1) * breadth] = part
        rim_ref[...] = jnp.concatenate(
            [side[i] for side in (before_ref, after_ref) for i in range(REACH)], axis=1
        )
        terms = slot_terms(
            weight_ref[...],
            offset_ref[...],
            cell_ref[...],
            counts_ref[...],
            start=start,
            breadth=breadth,
        )
        for k, term in enumerate(terms):
            term_ref[k] = term

    rim = rim_ref[...]
    make = functools.partial(slot_records, fields=fields, height=height, breadth=breadth)
    take = lambda k, b: term_ref[k, pl.ds(step * batch + b, 1), :]
    if start == 0:
        terms = [
            jnp.concatenate([take(k, b) for b in range(batch)], axis=1) for k in range(TERMS)
        ]
        made = make(terms, full_ref, rim)
        for b in range(batch):
            out_ref[b] = made[:, b * slots : (b + 1) * slots]
    else:
        for b in range(batch):
            alive = count_ref[step * batch + b] > start

            @pl.when(alive)
            def compute():
                out_ref[b] = make([take(k, b) for k in range(TERMS)], full_ref, rim)

            @pl.when(jnp.logical_not(alive))
            def clear():
                out_ref[b] = jnp.zeros((fields, slots), out_ref.dtype)


def deposit_part(record_ref, target_ref, *, highs, padded):
    batch, fields, _ = record_ref.shape
    target = jnp.concatenate([target_ref[b] for b in range(batch)], axis=1)
    values = jnp.concatenate([record_ref[b] for b in range(batch)], axis=1).astype(jnp.float32)
    slots = target.shape[1]
    values = jnp.concatenate(
        [values, jnp.zeros((padded - fields, slots), jnp.float32)], axis=0
    ).astype(jnp.bfloat16)
    high = target // LOW
    low = target - high * LOW
    spread = jnp.concatenate(
        [values * jnp.where(high == h, 1.0, 0.0).astype(jnp.bfloat16) for h in range(highs)],
        axis=0,
    )
    place = jnp.where(
        lax.broadcasted_iota(jnp.int32, (LOW, slots), 0) == low, 1.0, 0.0
    ).astype(jnp.bfloat16)
    return lax.dot_general(
        spread, place, (((1,), (1,)), ((), ())), preferred_element_type=jnp.float32
    )


def deposit_first_body(record_ref, target_ref, total_ref, *, highs, padded):
    part = deposit_part(record_ref, target_ref, highs=highs, padded=padded)

    @pl.when(pl.program_id(0) == 0)
    def first():
        total_ref[...] = part

    @pl.when(pl.program_id(0) > 0)
    def later():
        total_ref[...] = total_ref[...] + part


def deposit_last_body(
    record_ref, target_ref, before_ref, area_ref, out_ref, total_ref, *, highs, padded
):
    step = pl.program_id(0)
    fields = out_ref.shape[0]
    part = deposit_part(record_ref, target_ref, highs=highs, padded=padded)

    @pl.when(step == 0)
    def first():
        total_ref[...] = before_ref[...] + part

    @pl.when(step > 0)
    def later():
        total_ref[...] = total_ref[...] + part

    @pl.when(step == pl.num_programs(0) - 1)
    def finish():
        for h in range(highs):
            area = area_ref[:, h * LOW : (h + 1) * LOW]
            out_ref[:, h * LOW : (h + 1) * LOW] = (
                total_ref[h * padded : h * padded + fields, :] / area
            ).astype(jnp.bfloat16)


def neighbours(first, last, axis, wrap):
    size = lax.axis_size(axis)
    up = [(i, (i + 1) % size) for i in range(size if wrap else size - 1)]
    down = [(j, i) for i, j in up]
    return (lax.ppermute(last, axis, up), lax.ppermute(first, axis, down))


def on_device(
    source_flux, gauss_weight, gauss_offset, slot_count, source_cell, target_cell, target_area
):
    fields, height, breadth = source_flux.shape
    members = lax.axis_size("blk")
    capacity = source_cell.shape[1]
    cells = target_area.shape[0]
    groups = height // GROUP
    span = GROUP + 2 * REACH
    points = gauss_weight.shape[0]
    rows = jnp.swapaxes(source_flux, 0, 1)
    above, below = neighbours(rows[:REACH], rows[height - REACH :], "panel", False)
    picks = np.zeros((2 * REACH, breadth), np.float32)
    for i in range(REACH):
        picks[i, i] = 1.0
        picks[REACH + i, breadth - REACH + i] = 1.0
    edges = lax.dot_general(
        jnp.asarray(picks, jnp.bfloat16),
        source_flux,
        (((1,), (2,)), ((), ())),
        preferred_element_type=jnp.float32,
    ).astype(jnp.bfloat16)
    before, after = neighbours(edges[:REACH], edges[REACH:], "blk", True)
    half = capacity // 2
    arrived = []
    for part in range(2):
        records = pl.pallas_call(
            functools.partial(record_body, start=part * half),
            grid_spec=pltpu.PrefetchScalarGridSpec(
                num_scalar_prefetch=1,
                grid=(members // OWNERS,),
                in_specs=[
                    pl.BlockSpec((height, fields, breadth), lambda i, n: (0, 0, 0)),
                    pl.BlockSpec((REACH, fields, breadth), lambda i, n: (0, 0, 0)),
                    pl.BlockSpec((REACH, fields, breadth), lambda i, n: (0, 0, 0)),
                    pl.BlockSpec((REACH, fields, height), lambda i, n: (0, 0, 0)),
                    pl.BlockSpec((REACH, fields, height), lambda i, n: (0, 0, 0)),
                    pl.BlockSpec((points, members, half), lambda i, n, part=part: (0, 0, part)),
                    pl.BlockSpec(
                        (2, points, members, half), lambda i, n, part=part: (0, 0, 0, part)
                    ),
                    pl.BlockSpec((members, half), lambda i, n, part=part: (0, part)),
                    pl.BlockSpec((members, 1), lambda i, n: (0, 0)),
                ],
                out_specs=pl.BlockSpec((OWNERS, fields, half), lambda i, n: (i, 0, 0)),
                scratch_shapes=[
                    pltpu.VMEM((groups * fields, span * breadth), jnp.bfloat16),
                    pltpu.VMEM((fields, 2 * REACH * height), jnp.bfloat16),
                    pltpu.VMEM((TERMS, members, half), jnp.float32),
                ],
            ),
            out_shape=jax.ShapeDtypeStruct((members, fields, half), jnp.bfloat16),
            name=f"records_{part}",
        )(
            slot_count,
            rows,
            above,
            below,
            before,
            after,
            gauss_weight,
            gauss_offset,
            source_cell,
            slot_count.reshape(members, 1),
        )
        arrived.append(lax.all_to_all(records, "blk", split_axis=0, concat_axis=0, tiled=True))
    highs = cells // LOW
    padded = -(-fields // 16) * 16
    targets = target_cell.reshape(members, 1, capacity)
    record_spec = pl.BlockSpec((BATCH, fields, half), lambda i: (i, 0, 0))
    total_spec = pl.BlockSpec((highs * padded, LOW), lambda i: (0, 0))
    before = pl.pallas_call(
        functools.partial(deposit_first_body, highs=highs, padded=padded),
        grid=(members // BATCH,),
        in_specs=[record_spec, pl.BlockSpec((BATCH, 1, half), lambda i: (i, 0, 0))],
        out_specs=total_spec,
        out_shape=jax.ShapeDtypeStruct((highs * padded, LOW), jnp.float32),
        name="deposit_0",
    )(arrived[0], targets)
    return pl.pallas_call(
        functools.partial(deposit_last_body, highs=highs, padded=padded),
        grid=(members // BATCH,),
        in_specs=[
            record_spec,
            pl.BlockSpec((BATCH, 1, half), lambda i: (i, 0, 1)),
            total_spec,
            pl.BlockSpec((1, cells), lambda i: (0, 0)),
        ],
        out_specs=pl.BlockSpec((fields, cells), lambda i: (0, 0)),
        out_shape=jax.ShapeDtypeStruct((fields, cells), jnp.bfloat16),
        scratch_shapes=[pltpu.VMEM((highs * padded, LOW), jnp.float32)],
        name="deposit_1",
    )(arrived[1], targets, before, target_area.reshape(1, cells))


def solution(mesh):
    placed = (
        P(None, "panel", "blk"),
        P(None, ("panel", "blk"), None),
        P(None, None, ("panel", "blk"), None),
        P(("panel", "blk")),
        P(("panel", "blk"), None),
        P(("panel", "blk"), None),
        P(("panel", "blk")),
    )
    return jax.shard_map(
        on_device, mesh=mesh, in_specs=placed, out_specs=P(None, ("panel", "blk")), check_vma=False
    )
```

```python
import functools

import jax
import jax.numpy as jnp
import numpy as np
from jax import lax
from jax.experimental import pallas as pl
from jax.experimental.pallas import tpu as pltpu
from jax.sharding import PartitionSpec as P

GROUP = 8
REACH = 2
LOW = 256
TERMS = 11
BATCH = 8
OWNERS = (8, 4)


def slot_records(terms, window_ref, rim, *, fields, height, breadth):
    groups = height // GROUP
    span = GROUP + 2 * REACH
    slots = terms[0].shape[1]
    scale = terms[0]
    row_taps = terms[1:5]
    col_taps = terms[5:9]
    row = terms[9].astype(jnp.int32)
    col = terms[10].astype(jnp.int32)
    shifts = (-2, -1, 1, 2)
    group = row // GROUP
    local = row - group * GROUP + REACH
    one = jnp.ones((), jnp.bfloat16)
    zero = jnp.zeros((), jnp.bfloat16)
    place = lax.broadcasted_iota(jnp.int32, (breadth, slots), 0).astype(jnp.float32)
    gap = place.astype(jnp.bfloat16) - terms[10].astype(jnp.bfloat16)
    here = jnp.where(gap == 0, one, zero)
    beside = jnp.zeros((breadth, slots), jnp.bfloat16)
    for shift, tap in zip(shifts, col_taps):
        beside = jnp.where(gap == shift, tap.astype(jnp.bfloat16), beside)
    away = lax.broadcasted_iota(jnp.int32, (2 * GROUP, slots), 0) - local
    centres = jnp.where(away == 0, 1.0, 0.0)
    weights = centres
    for shift, tap in zip(shifts, row_taps):
        weights = jnp.where(away == shift, tap, weights)
    pieces = []
    for j in range(span):
        weight = weights[j : j + 1].astype(jnp.bfloat16)
        centre = centres[j : j + 1].astype(jnp.bfloat16)
        pieces.append(here * weight + beside * centre)
    table = jnp.concatenate(pieces, axis=0)
    product = jnp.dot(window_ref[...], table, preferred_element_type=jnp.float32)
    same_row = jnp.where(
        place[:height].astype(jnp.bfloat16) == terms[9].astype(jnp.bfloat16), one, zero
    )
    side = lax.broadcasted_iota(jnp.int32, (GROUP, slots), 0)
    reach = jnp.where(side < REACH, side - REACH, side + (breadth - REACH)) - col
    outer = jnp.zeros((GROUP, slots), jnp.float32)
    for shift, tap in zip(shifts, col_taps):
        outer = jnp.where(reach == shift, tap, outer)
    rim_pieces = [same_row * outer[i : i + 1].astype(jnp.bfloat16) for i in range(2 * REACH)]
    total = jnp.dot(rim, jnp.concatenate(rim_pieces, axis=0), preferred_element_type=jnp.float32)
    for g in range(groups):
        total = total + jnp.where(group == g, product[g * fields : (g + 1) * fields], 0.0)
    return (total * scale).astype(jnp.bfloat16)


def slot_terms(weight, offset, cell, count, *, start, breadth):
    offset_x = offset[0]
    offset_y = offset[1]
    slots = lax.broadcasted_iota(jnp.int32, cell.shape, 1) + start
    live = jnp.where(slots < count, 1.0, 0.0)
    area = jnp.sum(weight, axis=0)
    first_x = jnp.sum(weight * offset_x, axis=0)
    first_y = jnp.sum(weight * offset_y, axis=0)
    second_x = 0.5 * jnp.sum(weight * offset_x * offset_x, axis=0)
    second_y = 0.5 * jnp.sum(weight * offset_y * offset_y, axis=0)
    centre = area - 2.5 * (second_x + second_y)
    inverse = 1.0 / (12.0 * centre)
    terms = [centre * live]
    for one, two in ((first_x, second_x), (first_y, second_y)):
        terms += [
            (one - two) * inverse,
            (16.0 * two - 8.0 * one) * inverse,
            (16.0 * two + 8.0 * one) * inverse,
            (-one - two) * inverse,
        ]
    row = cell // breadth
    col = cell - row * breadth
    return terms + [row.astype(jnp.float32), col.astype(jnp.float32)]


def record_body(
    count_ref,
    rows_ref,
    above_ref,
    below_ref,
    before_ref,
    after_ref,
    weight_ref,
    offset_ref,
    cell_ref,
    counts_ref,
    out_ref,
    full_ref,
    rim_ref,
    term_ref,
    *,
    start,
):
    step = pl.program_id(0)
    height, fields, breadth = rows_ref.shape
    batch, _, slots = out_ref.shape

    @pl.when(step == 0)
    def fill():
        for g in range(height // GROUP):
            for j in range(GROUP + 2 * REACH):
                r = g * GROUP + j - REACH
                if r < 0:
                    part = above_ref[r + REACH]
                elif r >= height:
                    part = below_ref[r - height]
                else:
                    part = rows_ref[r]
                full_ref[g * fields : (g + 1) * fields, j * breadth : (j + 1) * breadth] = part
        rim_ref[...] = jnp.concatenate(
            [side[i] for side in (before_ref, after_ref) for i in range(REACH)], axis=1
        )
        terms = slot_terms(
            weight_ref[...],
            offset_ref[...],
            cell_ref[...],
            counts_ref[...],
            start=start,
            breadth=breadth,
        )
        for k, term in enumerate(terms):
            term_ref[k] = term

    rim = rim_ref[...]
    make = functools.partial(slot_records, fields=fields, height=height, breadth=breadth)
    take = lambda k, b: term_ref[k, pl.ds(step * batch + b, 1), :]
    if start == 0:
        terms = [
            jnp.concatenate([take(k, b) for b in range(batch)], axis=1) for k in range(TERMS)
        ]
        made = make(terms, full_ref, rim)
        for b in range(batch):
            out_ref[b] = made[:, b * slots : (b + 1) * slots]
    else:
        for b in range(batch):
            alive = count_ref[step * batch + b] > start

            @pl.when(alive)
            def compute():
                out_ref[b] = make([take(k, b) for k in range(TERMS)], full_ref, rim)

            @pl.when(jnp.logical_not(alive))
            def clear():
                out_ref[b] = jnp.zeros((fields, slots), out_ref.dtype)


def deposit_part(record_ref, target_ref, *, highs, padded, start):
    step = pl.program_id(0)
    _, fields, half = record_ref.shape
    sources = [step * BATCH + b for b in range(BATCH)]
    target = jnp.concatenate(
        [target_ref[pl.ds(k, 1), start : start + half] for k in sources], axis=1
    )
    values = jnp.concatenate([record_ref[k] for k in sources], axis=1).astype(jnp.float32)
    slots = target.shape[1]
    values = jnp.concatenate(
        [values, jnp.zeros((padded - fields, slots), jnp.float32)], axis=0
    ).astype(jnp.bfloat16)
    high = target // LOW
    low = (target - high * LOW).astype(jnp.float32).astype(jnp.bfloat16)
    spread = jnp.concatenate(
        [values * jnp.where(high == h, 1.0, 0.0).astype(jnp.bfloat16) for h in range(highs)],
        axis=0,
    )
    lane = lax.broadcasted_iota(jnp.int32, (LOW, slots), 0).astype(jnp.float32)
    place = jnp.where(
        lane.astype(jnp.bfloat16) == low, jnp.ones((), jnp.bfloat16), jnp.zeros((), jnp.bfloat16)
    )
    return lax.dot_general(
        spread, place, (((1,), (1,)), ((), ())), preferred_element_type=jnp.float32
    )


def deposit_first_body(record_ref, target_ref, total_ref, *, highs, padded):
    part = deposit_part(record_ref, target_ref, highs=highs, padded=padded, start=0)

    @pl.when(pl.program_id(0) == 0)
    def first():
        total_ref[...] = part

    @pl.when(pl.program_id(0) > 0)
    def later():
        total_ref[...] = total_ref[...] + part


def deposit_last_body(
    record_ref, target_ref, before_ref, area_ref, out_ref, total_ref, *, highs, padded
):
    step = pl.program_id(0)
    last = pl.num_programs(0) - 1
    fields = out_ref.shape[0]
    part = deposit_part(
        record_ref, target_ref, highs=highs, padded=padded, start=record_ref.shape[2]
    )

    @pl.when(step == 0)
    def first():
        total_ref[...] = before_ref[...] + part

    @pl.when(jnp.logical_and(step > 0, step < last))
    def later():
        total_ref[...] = total_ref[...] + part

    @pl.when(step == last)
    def finish():
        for h in range(highs):
            cut = slice(h * padded, h * padded + fields)
            inverse = 1.0 / area_ref[:, h * LOW : (h + 1) * LOW]
            out_ref[:, h * LOW : (h + 1) * LOW] = (
                (total_ref[cut, :] + part[cut]) * inverse
            ).astype(jnp.bfloat16)


def neighbours(first, last, axis, wrap):
    size = lax.axis_size(axis)
    up = [(i, (i + 1) % size) for i in range(size if wrap else size - 1)]
    down = [(j, i) for i, j in up]
    return (lax.ppermute(last, axis, up), lax.ppermute(first, axis, down))


def on_device(
    source_flux, gauss_weight, gauss_offset, slot_count, source_cell, target_cell, target_area
):
    fields, height, breadth = source_flux.shape
    members = lax.axis_size("blk")
    capacity = source_cell.shape[1]
    cells = target_area.shape[0]
    groups = height // GROUP
    span = GROUP + 2 * REACH
    points = gauss_weight.shape[0]
    rows = jnp.swapaxes(source_flux, 0, 1)
    above, below = neighbours(rows[:REACH], rows[height - REACH :], "panel", False)
    picks = np.zeros((2 * REACH, breadth), np.float32)
    for i in range(REACH):
        picks[i, i] = 1.0
        picks[REACH + i, breadth - REACH + i] = 1.0
    edges = lax.dot_general(
        jnp.asarray(picks, jnp.bfloat16),
        source_flux,
        (((1,), (2,)), ((), ())),
        preferred_element_type=jnp.float32,
    ).astype(jnp.bfloat16)
    before, after = neighbours(edges[:REACH], edges[REACH:], "blk", True)
    half = capacity // 2
    arrived = []
    for part, owners in enumerate(OWNERS):
        records = pl.pallas_call(
            functools.partial(record_body, start=part * half),
            grid_spec=pltpu.PrefetchScalarGridSpec(
                num_scalar_prefetch=1,
                grid=(members // owners,),
                in_specs=[
                    pl.BlockSpec((height, fields, breadth), lambda i, n: (0, 0, 0)),
                    pl.BlockSpec((REACH, fields, breadth), lambda i, n: (0, 0, 0)),
                    pl.BlockSpec((REACH, fields, breadth), lambda i, n: (0, 0, 0)),
                    pl.BlockSpec((REACH, fields, height), lambda i, n: (0, 0, 0)),
                    pl.BlockSpec((REACH, fields, height), lambda i, n: (0, 0, 0)),
                    pl.BlockSpec((points, members, half), lambda i, n, part=part: (0, 0, part)),
                    pl.BlockSpec(
                        (2, points, members, half), lambda i, n, part=part: (0, 0, 0, part)
                    ),
                    pl.BlockSpec((members, half), lambda i, n, part=part: (0, part)),
                    pl.BlockSpec((members, 1), lambda i, n: (0, 0)),
                ],
                out_specs=pl.BlockSpec((owners, fields, half), lambda i, n: (i, 0, 0)),
                scratch_shapes=[
                    pltpu.VMEM((groups * fields, span * breadth), jnp.bfloat16),
                    pltpu.VMEM((fields, 2 * REACH * height), jnp.bfloat16),
                    pltpu.VMEM((TERMS, members, half), jnp.float32),
                ],
            ),
            out_shape=jax.ShapeDtypeStruct((members, fields, half), jnp.bfloat16),
            name=f"records_{part}",
        )(
            slot_count,
            rows,
            above,
            below,
            before,
            after,
            gauss_weight,
            gauss_offset,
            source_cell,
            slot_count.reshape(members, 1),
        )
        arrived.append(lax.all_to_all(records, "blk", split_axis=0, concat_axis=0, tiled=True))
    highs = cells // LOW
    padded = -(-fields // 16) * 16
    record_spec = pl.BlockSpec(memory_space=pltpu.VMEM)
    target_spec = pl.BlockSpec((members, capacity), lambda i: (0, 0))
    total_spec = pl.BlockSpec((highs * padded, LOW), lambda i: (0, 0))
    before = pl.pallas_call(
        functools.partial(deposit_first_body, highs=highs, padded=padded),
        grid=(members // BATCH,),
        in_specs=[record_spec, target_spec],
        out_specs=total_spec,
        out_shape=jax.ShapeDtypeStruct((highs * padded, LOW), jnp.float32),
        name="deposit_0",
    )(arrived[0], target_cell)
    return pl.pallas_call(
        functools.partial(deposit_last_body, highs=highs, padded=padded),
        grid=(members // BATCH,),
        in_specs=[
            record_spec,
            target_spec,
            total_spec,
            pl.BlockSpec((1, cells), lambda i: (0, 0)),
        ],
        out_specs=pl.BlockSpec((fields, cells), lambda i: (0, 0)),
        out_shape=jax.ShapeDtypeStruct((fields, cells), jnp.bfloat16),
        scratch_shapes=[pltpu.VMEM((highs * padded, LOW), jnp.float32)],
        name="deposit_1",
    )(arrived[1], target_cell, before, target_area.reshape(1, cells))


def solution(mesh):
    placed = (
        P(None, "panel", "blk"),
        P(None, ("panel", "blk"), None),
        P(None, None, ("panel", "blk"), None),
        P(("panel", "blk")),
        P(("panel", "blk"), None),
        P(("panel", "blk"), None),
        P(("panel", "blk")),
    )
    return jax.shard_map(
        on_device, mesh=mesh, in_specs=placed, out_specs=P(None, ("panel", "blk")), check_vma=False
    )
```

```python
import functools

import jax
import jax.numpy as jnp
import numpy as np
from jax import lax
from jax.experimental import pallas as pl
from jax.experimental.pallas import tpu as pltpu
from jax.sharding import PartitionSpec as P

GROUP = 8
REACH = 2
LOW = 256
INNER = 4
TERMS = 11
BATCH = 8
OWNERS = (8, 4)


def slot_records(terms, window_ref, rim, *, fields, height, breadth):
    groups = height // GROUP
    span = GROUP + 2 * REACH
    slots = terms[0].shape[1]
    scale = terms[0]
    row_taps = terms[1:5]
    col_taps = terms[5:9]
    row = terms[9].astype(jnp.int32)
    col = terms[10].astype(jnp.int32)
    shifts = (-2, -1, 1, 2)
    group = row // GROUP
    local = row - group * GROUP + REACH
    one = jnp.ones((), jnp.bfloat16)
    zero = jnp.zeros((), jnp.bfloat16)
    place = lax.broadcasted_iota(jnp.int32, (breadth, slots), 0).astype(jnp.float32)
    gap = place.astype(jnp.bfloat16) - terms[10].astype(jnp.bfloat16)
    here = jnp.where(gap == 0, one, zero)
    beside = jnp.zeros((breadth, slots), jnp.bfloat16)
    for shift, tap in zip(shifts, col_taps):
        beside = jnp.where(gap == shift, tap.astype(jnp.bfloat16), beside)
    away = lax.broadcasted_iota(jnp.int32, (2 * GROUP, slots), 0) - local
    centres = jnp.where(away == 0, 1.0, 0.0)
    weights = centres
    for shift, tap in zip(shifts, row_taps):
        weights = jnp.where(away == shift, tap, weights)
    pieces = []
    for j in range(span):
        weight = weights[j : j + 1].astype(jnp.bfloat16)
        centre = centres[j : j + 1].astype(jnp.bfloat16)
        pieces.append(here * weight + beside * centre)
    table = jnp.concatenate(pieces, axis=0)
    product = jnp.dot(window_ref[...], table, preferred_element_type=jnp.float32)
    same_row = jnp.where(
        place[:height].astype(jnp.bfloat16) == terms[9].astype(jnp.bfloat16), one, zero
    )
    side = lax.broadcasted_iota(jnp.int32, (GROUP, slots), 0)
    reach = jnp.where(side < REACH, side - REACH, side + (breadth - REACH)) - col
    outer = jnp.zeros((GROUP, slots), jnp.float32)
    for shift, tap in zip(shifts, col_taps):
        outer = jnp.where(reach == shift, tap, outer)
    rim_pieces = [same_row * outer[i : i + 1].astype(jnp.bfloat16) for i in range(2 * REACH)]
    total = jnp.dot(rim, jnp.concatenate(rim_pieces, axis=0), preferred_element_type=jnp.float32)
    for g in range(groups):
        total = total + jnp.where(group == g, product[g * fields : (g + 1) * fields], 0.0)
    return (total * scale).astype(jnp.bfloat16)


def slot_terms(weight, offset, cell, count, *, start, breadth):
    offset_x = offset[0]
    offset_y = offset[1]
    slots = lax.broadcasted_iota(jnp.int32, cell.shape, 1) + start
    live = jnp.where(slots < count, 1.0, 0.0)
    area = jnp.sum(weight, axis=0)
    first_x = jnp.sum(weight * offset_x, axis=0)
    first_y = jnp.sum(weight * offset_y, axis=0)
    second_x = 0.5 * jnp.sum(weight * offset_x * offset_x, axis=0)
    second_y = 0.5 * jnp.sum(weight * offset_y * offset_y, axis=0)
    centre = area - 2.5 * (second_x + second_y)
    inverse = 1.0 / (12.0 * centre)
    terms = [centre * live]
    for one, two in ((first_x, second_x), (first_y, second_y)):
        terms += [
            (one - two) * inverse,
            (16.0 * two - 8.0 * one) * inverse,
            (16.0 * two + 8.0 * one) * inverse,
            (-one - two) * inverse,
        ]
    row = cell // breadth
    col = cell - row * breadth
    return terms + [row.astype(jnp.float32), col.astype(jnp.float32)]


def record_body(
    count_ref,
    rows_ref,
    above_ref,
    below_ref,
    before_ref,
    after_ref,
    weight_ref,
    offset_ref,
    cell_ref,
    out_ref,
    full_ref,
    rim_ref,
    term_ref,
    *,
    start,
):
    step = pl.program_id(0)
    height, fields, breadth = rows_ref.shape
    batch, _, slots = out_ref.shape

    @pl.when(step == 0)
    def fill():
        for g in range(height // GROUP):
            for j in range(GROUP + 2 * REACH):
                r = g * GROUP + j - REACH
                if r < 0:
                    part = above_ref[r + REACH]
                elif r >= height:
                    part = below_ref[r - height]
                else:
                    part = rows_ref[r]
                full_ref[g * fields : (g + 1) * fields, j * breadth : (j + 1) * breadth] = part
        rim_ref[...] = jnp.concatenate(
            [side[i] for side in (before_ref, after_ref) for i in range(REACH)], axis=1
        )
        member = lax.broadcasted_iota(jnp.int32, cell_ref.shape, 0)
        count = jnp.zeros(cell_ref.shape, jnp.int32)
        for m in range(cell_ref.shape[0]):
            count = jnp.where(member == m, count_ref[m], count)
        terms = slot_terms(
            weight_ref[...],
            offset_ref[...],
            cell_ref[...],
            count,
            start=start,
            breadth=breadth,
        )
        for k, term in enumerate(terms):
            term_ref[k] = term

    rim = rim_ref[...]
    make = functools.partial(slot_records, fields=fields, height=height, breadth=breadth)
    take = lambda k, b: term_ref[k, pl.ds(step * batch + b, 1), :]
    if start == 0:
        terms = [
            jnp.concatenate([take(k, b) for b in range(batch)], axis=1) for k in range(TERMS)
        ]
        made = make(terms, full_ref, rim)
        for b in range(batch):
            out_ref[b] = made[:, b * slots : (b + 1) * slots]
    else:
        for b in range(batch):
            alive = count_ref[step * batch + b] > start

            @pl.when(alive)
            def compute():
                out_ref[b] = make([take(k, b) for k in range(TERMS)], full_ref, rim)

            @pl.when(jnp.logical_not(alive))
            def clear():
                out_ref[b] = jnp.zeros((fields, slots), out_ref.dtype)


def deposit_part(record_ref, target_ref, *, highs, padded, start):
    step = pl.program_id(0)
    _, fields, half = record_ref.shape
    sources = [step * BATCH + b for b in range(BATCH)]
    target = jnp.concatenate(
        [target_ref[pl.ds(k, 1), start : start + half] for k in sources], axis=1
    )
    values = jnp.concatenate([record_ref[k] for k in sources], axis=1).astype(jnp.float32)
    slots = target.shape[1]
    values = jnp.concatenate(
        [values, jnp.zeros((padded - fields, slots), jnp.float32)], axis=0
    ).astype(jnp.bfloat16)
    high = target // LOW
    low = (target - high * LOW).astype(jnp.float32).astype(jnp.bfloat16)
    spread = jnp.concatenate(
        [values * jnp.where(high == h, 1.0, 0.0).astype(jnp.bfloat16) for h in range(highs)],
        axis=0,
    )
    lane = lax.broadcasted_iota(jnp.int32, (LOW, slots), 0).astype(jnp.float32)
    place = jnp.where(
        lane.astype(jnp.bfloat16) == low, jnp.ones((), jnp.bfloat16), jnp.zeros((), jnp.bfloat16)
    )
    return lax.dot_general(
        spread, place, (((1,), (1,)), ((), ())), preferred_element_type=jnp.float32
    )


def deposit_first_body(record_ref, target_ref, total_ref, *, highs, padded):
    part = deposit_part(record_ref, target_ref, highs=highs, padded=padded, start=0)

    @pl.when(pl.program_id(0) == 0)
    def first():
        total_ref[...] = part

    @pl.when(pl.program_id(0) > 0)
    def later():
        total_ref[...] = total_ref[...] + part


def deposit_last_body(
    record_ref, target_ref, before_ref, area_ref, out_ref, total_ref, *, highs, padded
):
    step = pl.program_id(0)
    last = pl.num_programs(0) - 1
    fields = out_ref.shape[0]
    part = deposit_part(
        record_ref, target_ref, highs=highs, padded=padded, start=record_ref.shape[2]
    )

    @pl.when(step == 0)
    def first():
        total_ref[...] = before_ref[...] + part

    @pl.when(jnp.logical_and(step > 0, step < last))
    def later():
        total_ref[...] = total_ref[...] + part

    @pl.when(step == last)
    def finish():
        for h in range(highs):
            cut = slice(h * padded, h * padded + fields)
            inverse = 1.0 / area_ref[:, h * LOW : (h + 1) * LOW]
            out_ref[:, h * LOW : (h + 1) * LOW] = (
                (total_ref[cut, :] + part[cut]) * inverse
            ).astype(jnp.bfloat16)


def neighbours(first, last, axis, wrap):
    size = lax.axis_size(axis)
    up = [(i, (i + 1) % size) for i in range(size if wrap else size - 1)]
    down = [(j, i) for i, j in up]
    return (lax.ppermute(last, axis, up), lax.ppermute(first, axis, down))


def ring_neighbours(first, last, axis):
    size = lax.axis_size(axis)
    inner = INNER if size % INNER == 0 and size > INNER else 1
    if inner == 1:
        return neighbours(first, last, axis, True)
    up = [(i, i // inner * inner + (i + 1) % inner) for i in range(size)]
    down = [(j, i) for i, j in up]
    before = lax.ppermute(last, axis, up)
    after = lax.ppermute(first, axis, down)
    head = [(i, (i + inner) % size) for i in range(0, size, inner)]
    tail = [(i, (i - inner) % size) for i in range(inner - 1, size, inner)]
    spot = lax.axis_index(axis) % inner
    turned = lax.ppermute(jnp.where(spot == 0, before, after), axis, head + tail)
    return (
        jnp.where(spot == 0, turned, before),
        jnp.where(spot == inner - 1, turned, after),
    )


def on_device(
    source_flux, gauss_weight, gauss_offset, slot_count, source_cell, target_cell, target_area
):
    fields, height, breadth = source_flux.shape
    members = lax.axis_size("blk")
    capacity = source_cell.shape[1]
    cells = target_area.shape[0]
    groups = height // GROUP
    span = GROUP + 2 * REACH
    points = gauss_weight.shape[0]
    rows = jnp.swapaxes(source_flux, 0, 1)
    above, below = neighbours(rows[:REACH], rows[height - REACH :], "panel", False)
    picks = np.zeros((2 * REACH, breadth), np.float32)
    for i in range(REACH):
        picks[i, i] = 1.0
        picks[REACH + i, breadth - REACH + i] = 1.0
    edges = lax.dot_general(
        jnp.asarray(picks, jnp.bfloat16),
        source_flux,
        (((1,), (2,)), ((), ())),
        preferred_element_type=jnp.float32,
    ).astype(jnp.bfloat16)
    before, after = ring_neighbours(edges[:REACH], edges[REACH:], "blk")
    half = capacity // 2
    arrived = []
    for part, owners in enumerate(OWNERS):
        records = pl.pallas_call(
            functools.partial(record_body, start=part * half),
            grid_spec=pltpu.PrefetchScalarGridSpec(
                num_scalar_prefetch=1,
                grid=(members // owners,),
                in_specs=[
                    pl.BlockSpec((height, fields, breadth), lambda i, n: (0, 0, 0)),
                    pl.BlockSpec((REACH, fields, breadth), lambda i, n: (0, 0, 0)),
                    pl.BlockSpec((REACH, fields, breadth), lambda i, n: (0, 0, 0)),
                    pl.BlockSpec((REACH, fields, height), lambda i, n: (0, 0, 0)),
                    pl.BlockSpec((REACH, fields, height), lambda i, n: (0, 0, 0)),
                    pl.BlockSpec((points, members, half), lambda i, n, part=part: (0, 0, part)),
                    pl.BlockSpec(
                        (2, points, members, half), lambda i, n, part=part: (0, 0, 0, part)
                    ),
                    pl.BlockSpec((members, half), lambda i, n, part=part: (0, part)),
                ],
                out_specs=pl.BlockSpec((owners, fields, half), lambda i, n: (i, 0, 0)),
                scratch_shapes=[
                    pltpu.VMEM((groups * fields, span * breadth), jnp.bfloat16),
                    pltpu.VMEM((fields, 2 * REACH * height), jnp.bfloat16),
                    pltpu.VMEM((TERMS, members, half), jnp.float32),
                ],
            ),
            out_shape=jax.ShapeDtypeStruct((members, fields, half), jnp.bfloat16),
            name=f"records_{part}",
        )(
            slot_count,
            rows,
            above,
            below,
            before,
            after,
            gauss_weight,
            gauss_offset,
            source_cell,
        )
        arrived.append(lax.all_to_all(records, "blk", split_axis=0, concat_axis=0, tiled=True))
    highs = cells // LOW
    padded = -(-fields // 16) * 16
    record_spec = pl.BlockSpec(memory_space=pltpu.VMEM)
    target_spec = pl.BlockSpec((members, capacity), lambda i: (0, 0))
    total_spec = pl.BlockSpec((highs * padded, LOW), lambda i: (0, 0))
    before = pl.pallas_call(
        functools.partial(deposit_first_body, highs=highs, padded=padded),
        grid=(members // BATCH,),
        in_specs=[record_spec, target_spec],
        out_specs=total_spec,
        out_shape=jax.ShapeDtypeStruct((highs * padded, LOW), jnp.float32),
        name="deposit_0",
    )(arrived[0], target_cell)
    return pl.pallas_call(
        functools.partial(deposit_last_body, highs=highs, padded=padded),
        grid=(members // BATCH,),
        in_specs=[
            record_spec,
            target_spec,
            total_spec,
            pl.BlockSpec((1, cells), lambda i: (0, 0)),
        ],
        out_specs=pl.BlockSpec((fields, cells), lambda i: (0, 0)),
        out_shape=jax.ShapeDtypeStruct((fields, cells), jnp.bfloat16),
        scratch_shapes=[pltpu.VMEM((highs * padded, LOW), jnp.float32)],
        name="deposit_1",
    )(arrived[1], target_cell, before, target_area.reshape(1, cells))


def solution(mesh):
    placed = (
        P(None, "panel", "blk"),
        P(None, ("panel", "blk"), None),
        P(None, None, ("panel", "blk"), None),
        P(("panel", "blk")),
        P(("panel", "blk"), None),
        P(("panel", "blk"), None),
        P(("panel", "blk")),
    )
    return jax.shard_map(
        on_device, mesh=mesh, in_specs=placed, out_specs=P(None, ("panel", "blk")), check_vma=False
    )
```

```python
import functools

import jax
import jax.numpy as jnp
import numpy as np
from jax import lax
from jax.experimental import pallas as pl
from jax.experimental.pallas import tpu as pltpu
from jax.sharding import PartitionSpec as P

GROUP = 8
REACH = 2
LOW = 256
TERMS = 11
BATCH = 8
SHIFTS = (-2, -1, 1, 2)


def window_sum(terms, window_ref, *, fields, breadth):
    span = GROUP + 2 * REACH
    slots = terms[0].shape[1]
    row = terms[9].astype(jnp.int32)
    group = row // GROUP
    local = row - group * GROUP + REACH
    one = jnp.ones((), jnp.bfloat16)
    zero = jnp.zeros((), jnp.bfloat16)
    place = lax.broadcasted_iota(jnp.int32, (breadth, slots), 0).astype(jnp.float32)
    gap = place.astype(jnp.bfloat16) - terms[10].astype(jnp.bfloat16)
    here = jnp.where(gap == 0, one, zero)
    beside = jnp.zeros((breadth, slots), jnp.bfloat16)
    for shift, tap in zip(SHIFTS, terms[5:9]):
        beside = jnp.where(gap == shift, tap.astype(jnp.bfloat16), beside)
    away = lax.broadcasted_iota(jnp.int32, (2 * GROUP, slots), 0) - local
    centres = jnp.where(away == 0, 1.0, 0.0)
    weights = centres
    for shift, tap in zip(SHIFTS, terms[1:5]):
        weights = jnp.where(away == shift, tap, weights)
    pieces = []
    for j in range(span):
        weight = weights[j : j + 1].astype(jnp.bfloat16)
        centre = centres[j : j + 1].astype(jnp.bfloat16)
        pieces.append(here * weight + beside * centre)
    table = jnp.concatenate(pieces, axis=0)
    product = jnp.dot(window_ref[...], table, preferred_element_type=jnp.float32)
    total = jnp.where(group == 0, product[:fields], 0.0)
    for g in range(1, product.shape[0] // fields):
        total = total + jnp.where(group == g, product[g * fields : (g + 1) * fields], 0.0)
    return total


def rim_sum(terms, rim, *, height, breadth):
    slots = terms[0].shape[1]
    col = terms[10].astype(jnp.int32)
    place = lax.broadcasted_iota(jnp.int32, (height, slots), 0).astype(jnp.float32)
    same_row = jnp.where(
        place.astype(jnp.bfloat16) == terms[9].astype(jnp.bfloat16),
        jnp.ones((), jnp.bfloat16),
        jnp.zeros((), jnp.bfloat16),
    )
    side = lax.broadcasted_iota(jnp.int32, (GROUP, slots), 0)
    reach = jnp.where(side < REACH, side - REACH, side + (breadth - REACH)) - col
    outer = jnp.zeros((GROUP, slots), jnp.float32)
    for shift, tap in zip(SHIFTS, terms[5:9]):
        outer = jnp.where(reach == shift, tap, outer)
    pieces = [same_row * outer[i : i + 1].astype(jnp.bfloat16) for i in range(2 * REACH)]
    return jnp.dot(rim, jnp.concatenate(pieces, axis=0), preferred_element_type=jnp.float32)


def slot_terms(weight, offset, cell, count, *, start, breadth):
    offset_x = offset[0]
    offset_y = offset[1]
    slots = lax.broadcasted_iota(jnp.int32, cell.shape, 1) + start
    live = jnp.where(slots < count, 1.0, 0.0)
    area = jnp.sum(weight, axis=0)
    first_x = jnp.sum(weight * offset_x, axis=0)
    first_y = jnp.sum(weight * offset_y, axis=0)
    second_x = 0.5 * jnp.sum(weight * offset_x * offset_x, axis=0)
    second_y = 0.5 * jnp.sum(weight * offset_y * offset_y, axis=0)
    centre = area - 2.5 * (second_x + second_y)
    inverse = 1.0 / (12.0 * centre)
    terms = [centre * live]
    for one, two in ((first_x, second_x), (first_y, second_y)):
        terms += [
            (one - two) * inverse,
            (16.0 * two - 8.0 * one) * inverse,
            (16.0 * two + 8.0 * one) * inverse,
            (-one - two) * inverse,
        ]
    row = cell // breadth
    col = cell - row * breadth
    return terms + [row.astype(jnp.float32), col.astype(jnp.float32)]


def fill_window(rows_ref, above_ref, below_ref, full_ref):
    height, fields, breadth = rows_ref.shape
    for g in range(height // GROUP):
        for j in range(GROUP + 2 * REACH):
            r = g * GROUP + j - REACH
            if r < 0:
                part = above_ref[r + REACH]
            elif r >= height:
                part = below_ref[r - height]
            else:
                part = rows_ref[r]
            full_ref[g * fields : (g + 1) * fields, j * breadth : (j + 1) * breadth] = part


def fill_rim(before_ref, after_ref, rim_ref):
    rim_ref[...] = jnp.concatenate(
        [side[i] for side in (before_ref, after_ref) for i in range(REACH)], axis=1
    )


def fill_terms(count_ref, weight_ref, offset_ref, cell_ref, term_ref, *, start, breadth):
    member = lax.broadcasted_iota(jnp.int32, cell_ref.shape, 0)
    count = jnp.zeros(cell_ref.shape, jnp.int32)
    for m in range(cell_ref.shape[0]):
        count = jnp.where(member == m, count_ref[m], count)
    terms = slot_terms(
        weight_ref[...], offset_ref[...], cell_ref[...], count, start=start, breadth=breadth
    )
    for k, term in enumerate(terms):
        term_ref[k] = term


def row_terms(term_ref, first, batch):
    return [
        jnp.concatenate([term_ref[k, pl.ds(first + b, 1), :] for b in range(batch)], axis=1)
        for k in range(TERMS)
    ]


def inner_body(
    count_ref,
    rows_ref,
    above_ref,
    below_ref,
    weight_ref,
    offset_ref,
    cell_ref,
    out_ref,
    full_ref,
    term_ref,
):
    step = pl.program_id(0)
    _, fields, breadth = rows_ref.shape
    batch, _, slots = out_ref.shape

    @pl.when(step == 0)
    def fill():
        fill_window(rows_ref, above_ref, below_ref, full_ref)
        fill_terms(
            count_ref, weight_ref, offset_ref, cell_ref, term_ref, start=0, breadth=breadth
        )

    made = window_sum(
        row_terms(term_ref, step * batch, batch), full_ref, fields=fields, breadth=breadth
    )
    for b in range(batch):
        out_ref[b] = made[:, b * slots : (b + 1) * slots]


def outer_body(
    count_ref,
    inner_ref,
    before_ref,
    after_ref,
    weight_ref,
    offset_ref,
    cell_ref,
    out_ref,
    rim_ref,
    term_ref,
    *,
    height,
    breadth,
):
    step = pl.program_id(0)
    batch, _, slots = out_ref.shape

    @pl.when(step == 0)
    def fill():
        fill_rim(before_ref, after_ref, rim_ref)
        fill_terms(
            count_ref, weight_ref, offset_ref, cell_ref, term_ref, start=0, breadth=breadth
        )

    terms = row_terms(term_ref, step * batch, batch)
    made = rim_sum(terms, rim_ref[...], height=height, breadth=breadth)
    for b in range(batch):
        cut = slice(b * slots, (b + 1) * slots)
        out_ref[b] = ((inner_ref[b] + made[:, cut]) * terms[0][:, cut]).astype(jnp.bfloat16)


def record_body(
    count_ref,
    rows_ref,
    above_ref,
    below_ref,
    before_ref,
    after_ref,
    weight_ref,
    offset_ref,
    cell_ref,
    out_ref,
    full_ref,
    rim_ref,
    term_ref,
    *,
    start,
):
    step = pl.program_id(0)
    height, fields, breadth = rows_ref.shape
    batch, _, slots = out_ref.shape

    @pl.when(step == 0)
    def fill():
        fill_window(rows_ref, above_ref, below_ref, full_ref)
        fill_rim(before_ref, after_ref, rim_ref)
        fill_terms(
            count_ref, weight_ref, offset_ref, cell_ref, term_ref, start=start, breadth=breadth
        )

    for b in range(batch):
        alive = count_ref[step * batch + b] > start

        @pl.when(alive)
        def compute():
            terms = row_terms(term_ref, step * batch + b, 1)
            total = window_sum(terms, full_ref, fields=fields, breadth=breadth)
            total = total + rim_sum(terms, rim_ref[...], height=height, breadth=breadth)
            out_ref[b] = (total * terms[0]).astype(jnp.bfloat16)

        @pl.when(jnp.logical_not(alive))
        def clear():
            out_ref[b] = jnp.zeros((fields, slots), out_ref.dtype)


def deposit_part(record_ref, target_ref, *, highs, padded, start):
    step = pl.program_id(0)
    _, fields, half = record_ref.shape
    sources = [step * BATCH + b for b in range(BATCH)]
    target = jnp.concatenate(
        [target_ref[pl.ds(k, 1), start : start + half] for k in sources], axis=1
    )
    values = jnp.concatenate([record_ref[k] for k in sources], axis=1).astype(jnp.float32)
    slots = target.shape[1]
    values = jnp.concatenate(
        [values, jnp.zeros((padded - fields, slots), jnp.float32)], axis=0
    ).astype(jnp.bfloat16)
    high = target // LOW
    low = (target - high * LOW).astype(jnp.float32).astype(jnp.bfloat16)
    spread = jnp.concatenate(
        [values * jnp.where(high == h, 1.0, 0.0).astype(jnp.bfloat16) for h in range(highs)],
        axis=0,
    )
    lane = lax.broadcasted_iota(jnp.int32, (LOW, slots), 0).astype(jnp.float32)
    place = jnp.where(
        lane.astype(jnp.bfloat16) == low, jnp.ones((), jnp.bfloat16), jnp.zeros((), jnp.bfloat16)
    )
    return lax.dot_general(
        spread, place, (((1,), (1,)), ((), ())), preferred_element_type=jnp.float32
    )


def deposit_first_body(record_ref, target_ref, total_ref, *, highs, padded):
    part = deposit_part(record_ref, target_ref, highs=highs, padded=padded, start=0)

    @pl.when(pl.program_id(0) == 0)
    def first():
        total_ref[...] = part

    @pl.when(pl.program_id(0) > 0)
    def later():
        total_ref[...] = total_ref[...] + part


def deposit_last_body(
    record_ref, target_ref, before_ref, area_ref, out_ref, total_ref, *, highs, padded
):
    step = pl.program_id(0)
    last = pl.num_programs(0) - 1
    fields = out_ref.shape[0]
    part = deposit_part(
        record_ref, target_ref, highs=highs, padded=padded, start=record_ref.shape[2]
    )

    @pl.when(step == 0)
    def first():
        total_ref[...] = before_ref[...] + part

    @pl.when(jnp.logical_and(step > 0, step < last))
    def later():
        total_ref[...] = total_ref[...] + part

    @pl.when(step == last)
    def finish():
        for h in range(highs):
            cut = slice(h * padded, h * padded + fields)
            inverse = 1.0 / area_ref[:, h * LOW : (h + 1) * LOW]
            out_ref[:, h * LOW : (h + 1) * LOW] = (
                (total_ref[cut, :] + part[cut]) * inverse
            ).astype(jnp.bfloat16)


def neighbours(first, last, axis, wrap):
    size = lax.axis_size(axis)
    up = [(i, (i + 1) % size) for i in range(size if wrap else size - 1)]
    down = [(j, i) for i, j in up]
    return (lax.ppermute(last, axis, up), lax.ppermute(first, axis, down))


def on_device(
    source_flux, gauss_weight, gauss_offset, slot_count, source_cell, target_cell, target_area
):
    fields, height, breadth = source_flux.shape
    members = lax.axis_size("blk")
    capacity = source_cell.shape[1]
    cells = target_area.shape[0]
    groups = height // GROUP
    span = GROUP + 2 * REACH
    points = gauss_weight.shape[0]
    rows = jnp.swapaxes(source_flux, 0, 1)
    above, below = neighbours(rows[:REACH], rows[height - REACH :], "panel", False)
    picks = np.zeros((2 * REACH, breadth), np.float32)
    for i in range(REACH):
        picks[i, i] = 1.0
        picks[REACH + i, breadth - REACH + i] = 1.0
    edges = lax.dot_general(
        jnp.asarray(picks, jnp.bfloat16),
        source_flux,
        (((1,), (2,)), ((), ())),
        preferred_element_type=jnp.float32,
    ).astype(jnp.bfloat16)
    before, after = neighbours(edges[:REACH], edges[REACH:], "blk", True)
    half = capacity // 2
    whole = lambda *shape: pl.BlockSpec(shape, lambda i, n: (0,) * len(shape))
    strip = lambda owners: pl.BlockSpec((owners, fields, half), lambda i, n: (i, 0, 0))
    row_specs = [whole(height, fields, breadth)] + [whole(REACH, fields, breadth)] * 2
    rim_specs = [whole(REACH, fields, height)] * 2

    def slot_specs(part):
        return [
            pl.BlockSpec((points, members, half), lambda i, n: (0, 0, part)),
            pl.BlockSpec((2, points, members, half), lambda i, n: (0, 0, 0, part)),
            pl.BlockSpec((members, half), lambda i, n: (0, part)),
        ]

    full = pltpu.VMEM((groups * fields, span * breadth), jnp.bfloat16)
    rim = pltpu.VMEM((fields, 2 * REACH * height), jnp.bfloat16)
    held = pltpu.VMEM((TERMS, members, half), jnp.float32)

    def call(body, owners, specs, scratch, dtype, name):
        return pl.pallas_call(
            body,
            grid_spec=pltpu.PrefetchScalarGridSpec(
                num_scalar_prefetch=1,
                grid=(members // owners,),
                in_specs=specs,
                out_specs=strip(owners),
                scratch_shapes=scratch,
            ),
            out_shape=jax.ShapeDtypeStruct((members, fields, half), dtype),
            name=name,
        )

    slot_inputs = (gauss_weight, gauss_offset, source_cell)
    inner = call(
        inner_body, 8, row_specs + slot_specs(0), [full, held], jnp.float32, "records_inner"
    )(slot_count, rows, above, below, *slot_inputs)
    early = call(
        functools.partial(outer_body, height=height, breadth=breadth),
        4,
        [strip(4)] + rim_specs + slot_specs(0),
        [rim, held],
        jnp.bfloat16,
        "records_outer",
    )(slot_count, inner, before, after, *slot_inputs)
    late = call(
        functools.partial(record_body, start=half),
        4,
        row_specs + rim_specs + slot_specs(1),
        [full, rim, held],
        jnp.bfloat16,
        "records_late",
    )(slot_count, rows, above, below, before, after, *slot_inputs)
    arrived = [
        lax.all_to_all(part, "blk", split_axis=0, concat_axis=0, tiled=True)
        for part in (early, late)
    ]
    highs = cells // LOW
    padded = -(-fields // 16) * 16
    record_spec = pl.BlockSpec(memory_space=pltpu.VMEM)
    target_spec = pl.BlockSpec((members, capacity), lambda i: (0, 0))
    total_spec = pl.BlockSpec((highs * padded, LOW), lambda i: (0, 0))
    before = pl.pallas_call(
        functools.partial(deposit_first_body, highs=highs, padded=padded),
        grid=(members // BATCH,),
        in_specs=[record_spec, target_spec],
        out_specs=total_spec,
        out_shape=jax.ShapeDtypeStruct((highs * padded, LOW), jnp.float32),
        name="deposit_0",
    )(arrived[0], target_cell)
    return pl.pallas_call(
        functools.partial(deposit_last_body, highs=highs, padded=padded),
        grid=(members // BATCH,),
        in_specs=[
            record_spec,
            target_spec,
            total_spec,
            pl.BlockSpec((1, cells), lambda i: (0, 0)),
        ],
        out_specs=pl.BlockSpec((fields, cells), lambda i: (0, 0)),
        out_shape=jax.ShapeDtypeStruct((fields, cells), jnp.bfloat16),
        scratch_shapes=[pltpu.VMEM((highs * padded, LOW), jnp.float32)],
        name="deposit_1",
    )(arrived[1], target_cell, before, target_area.reshape(1, cells))


def solution(mesh):
    placed = (
        P(None, "panel", "blk"),
        P(None, ("panel", "blk"), None),
        P(None, None, ("panel", "blk"), None),
        P(("panel", "blk")),
        P(("panel", "blk"), None),
        P(("panel", "blk"), None),
        P(("panel", "blk")),
    )
    return jax.shard_map(
        on_device, mesh=mesh, in_specs=placed, out_specs=P(None, ("panel", "blk")), check_vma=False
    )
```

```python
import functools

import jax
import jax.numpy as jnp
import numpy as np
from jax import lax
from jax.experimental import pallas as pl
from jax.experimental.pallas import tpu as pltpu
from jax.sharding import PartitionSpec as P

GROUP = 8
REACH = 2
LOW = 256
TERMS = 11
BATCH = 8
OWNERS = (8, 4)


def slot_records(terms, window_ref, rim, *, fields, height, breadth):
    groups = height // GROUP
    span = GROUP + 2 * REACH
    slots = terms[0].shape[1]
    scale = terms[0]
    row_taps = terms[1:5]
    col_taps = terms[5:9]
    row = terms[9].astype(jnp.int32)
    col = terms[10].astype(jnp.int32)
    shifts = (-2, -1, 1, 2)
    group = row // GROUP
    local = row - group * GROUP + REACH
    one = jnp.ones((), jnp.bfloat16)
    zero = jnp.zeros((), jnp.bfloat16)
    place = lax.broadcasted_iota(jnp.int32, (breadth, slots), 0).astype(jnp.float32)
    gap = place.astype(jnp.bfloat16) - terms[10].astype(jnp.bfloat16)
    here = jnp.where(gap == 0, one, zero)
    beside = jnp.zeros((breadth, slots), jnp.bfloat16)
    for shift, tap in zip(shifts, col_taps):
        beside = jnp.where(gap == shift, tap.astype(jnp.bfloat16), beside)
    away = lax.broadcasted_iota(jnp.int32, (2 * GROUP, slots), 0) - local
    centres = jnp.where(away == 0, 1.0, 0.0)
    weights = centres
    for shift, tap in zip(shifts, row_taps):
        weights = jnp.where(away == shift, tap, weights)
    pieces = []
    for j in range(span):
        weight = weights[j : j + 1].astype(jnp.bfloat16)
        centre = centres[j : j + 1].astype(jnp.bfloat16)
        pieces.append(here * weight + beside * centre)
    table = jnp.concatenate(pieces, axis=0)
    product = jnp.dot(window_ref[...], table, preferred_element_type=jnp.float32)
    same_row = jnp.where(
        place[:height].astype(jnp.bfloat16) == terms[9].astype(jnp.bfloat16), one, zero
    )
    side = lax.broadcasted_iota(jnp.int32, (GROUP, slots), 0)
    reach = jnp.where(side < REACH, side - REACH, side + (breadth - REACH)) - col
    outer = jnp.zeros((GROUP, slots), jnp.float32)
    for shift, tap in zip(shifts, col_taps):
        outer = jnp.where(reach == shift, tap, outer)
    rim_pieces = [same_row * outer[i : i + 1].astype(jnp.bfloat16) for i in range(2 * REACH)]
    total = jnp.dot(rim, jnp.concatenate(rim_pieces, axis=0), preferred_element_type=jnp.float32)
    for g in range(groups):
        total = total + jnp.where(group == g, product[g * fields : (g + 1) * fields], 0.0)
    return (total * scale).astype(jnp.bfloat16)


def slot_terms(weight, offset, cell, count, *, start, breadth):
    offset_x = offset[0]
    offset_y = offset[1]
    slots = lax.broadcasted_iota(jnp.int32, cell.shape, 1) + start
    live = jnp.where(slots < count, 1.0, 0.0)
    area = jnp.sum(weight, axis=0)
    first_x = jnp.sum(weight * offset_x, axis=0)
    first_y = jnp.sum(weight * offset_y, axis=0)
    second_x = 0.5 * jnp.sum(weight * offset_x * offset_x, axis=0)
    second_y = 0.5 * jnp.sum(weight * offset_y * offset_y, axis=0)
    centre = area - 2.5 * (second_x + second_y)
    inverse = 1.0 / (12.0 * centre)
    terms = [centre * live]
    for one, two in ((first_x, second_x), (first_y, second_y)):
        terms += [
            (one - two) * inverse,
            (16.0 * two - 8.0 * one) * inverse,
            (16.0 * two + 8.0 * one) * inverse,
            (-one - two) * inverse,
        ]
    row = cell // breadth
    col = cell - row * breadth
    return terms + [row.astype(jnp.float32), col.astype(jnp.float32)]


def record_body(
    count_ref,
    rows_ref,
    above_ref,
    below_ref,
    beside_ref,
    weight_ref,
    offset_ref,
    cell_ref,
    out_ref,
    full_ref,
    rim_ref,
    term_ref,
    *,
    start,
):
    step = pl.program_id(0)
    height, fields, breadth = rows_ref.shape
    batch, _, slots = out_ref.shape

    @pl.when(step == 0)
    def fill():
        for g in range(height // GROUP):
            for j in range(GROUP + 2 * REACH):
                r = g * GROUP + j - REACH
                if r < 0:
                    part = above_ref[r + REACH]
                elif r >= height:
                    part = below_ref[r - height]
                else:
                    part = rows_ref[r]
                full_ref[g * fields : (g + 1) * fields, j * breadth : (j + 1) * breadth] = part
        rim_ref[...] = jnp.concatenate(
            [beside_ref[i] for i in range(2 * REACH)], axis=1
        )
        member = lax.broadcasted_iota(jnp.int32, cell_ref.shape, 0)
        count = jnp.zeros(cell_ref.shape, jnp.int32)
        for m in range(cell_ref.shape[0]):
            count = jnp.where(member == m, count_ref[m], count)
        terms = slot_terms(
            weight_ref[...],
            offset_ref[...],
            cell_ref[...],
            count,
            start=start,
            breadth=breadth,
        )
        for k, term in enumerate(terms):
            term_ref[k] = term

    rim = rim_ref[...]
    make = functools.partial(slot_records, fields=fields, height=height, breadth=breadth)
    take = lambda k, b: term_ref[k, pl.ds(step * batch + b, 1), :]
    if start == 0:
        terms = [
            jnp.concatenate([take(k, b) for b in range(batch)], axis=1) for k in range(TERMS)
        ]
        made = make(terms, full_ref, rim)
        for b in range(batch):
            out_ref[b] = made[:, b * slots : (b + 1) * slots]
    else:
        for b in range(batch):
            alive = count_ref[step * batch + b] > start

            @pl.when(alive)
            def compute():
                out_ref[b] = make([take(k, b) for k in range(TERMS)], full_ref, rim)

            @pl.when(jnp.logical_not(alive))
            def clear():
                out_ref[b] = jnp.zeros((fields, slots), out_ref.dtype)


def deposit_part(record_ref, target_ref, *, highs, padded, start):
    step = pl.program_id(0)
    _, fields, half = record_ref.shape
    sources = [step * BATCH + b for b in range(BATCH)]
    target = jnp.concatenate(
        [target_ref[pl.ds(k, 1), start : start + half] for k in sources], axis=1
    )
    values = jnp.concatenate([record_ref[k] for k in sources], axis=1).astype(jnp.float32)
    slots = target.shape[1]
    values = jnp.concatenate(
        [values, jnp.zeros((padded - fields, slots), jnp.float32)], axis=0
    ).astype(jnp.bfloat16)
    high = target // LOW
    low = (target - high * LOW).astype(jnp.float32).astype(jnp.bfloat16)
    spread = jnp.concatenate(
        [values * jnp.where(high == h, 1.0, 0.0).astype(jnp.bfloat16) for h in range(highs)],
        axis=0,
    )
    lane = lax.broadcasted_iota(jnp.int32, (LOW, slots), 0).astype(jnp.float32)
    place = jnp.where(
        lane.astype(jnp.bfloat16) == low, jnp.ones((), jnp.bfloat16), jnp.zeros((), jnp.bfloat16)
    )
    return lax.dot_general(
        spread, place, (((1,), (1,)), ((), ())), preferred_element_type=jnp.float32
    )


def deposit_first_body(record_ref, target_ref, total_ref, *, highs, padded):
    part = deposit_part(record_ref, target_ref, highs=highs, padded=padded, start=0)

    @pl.when(pl.program_id(0) == 0)
    def first():
        total_ref[...] = part

    @pl.when(pl.program_id(0) > 0)
    def later():
        total_ref[...] = total_ref[...] + part


def deposit_last_body(
    record_ref, target_ref, before_ref, area_ref, out_ref, total_ref, *, highs, padded
):
    step = pl.program_id(0)
    last = pl.num_programs(0) - 1
    fields = out_ref.shape[0]
    part = deposit_part(
        record_ref, target_ref, highs=highs, padded=padded, start=record_ref.shape[2]
    )

    @pl.when(step == 0)
    def first():
        total_ref[...] = before_ref[...] + part

    @pl.when(jnp.logical_and(step > 0, step < last))
    def later():
        total_ref[...] = total_ref[...] + part

    @pl.when(step == last)
    def finish():
        for h in range(highs):
            cut = slice(h * padded, h * padded + fields)
            inverse = 1.0 / area_ref[:, h * LOW : (h + 1) * LOW]
            out_ref[:, h * LOW : (h + 1) * LOW] = (
                (total_ref[cut, :] + part[cut]) * inverse
            ).astype(jnp.bfloat16)


def neighbours(first, last, axis, wrap):
    size = lax.axis_size(axis)
    up = [(i, (i + 1) % size) for i in range(size if wrap else size - 1)]
    down = [(j, i) for i, j in up]
    return (lax.ppermute(last, axis, up), lax.ppermute(first, axis, down))


def on_device(
    source_flux, gauss_weight, gauss_offset, slot_count, source_cell, target_cell, target_area
):
    fields, height, breadth = source_flux.shape
    members = lax.axis_size("blk")
    capacity = source_cell.shape[1]
    cells = target_area.shape[0]
    groups = height // GROUP
    span = GROUP + 2 * REACH
    points = gauss_weight.shape[0]
    picks = np.zeros((2 * REACH, breadth), np.float32)
    for i in range(REACH):
        picks[i, i] = 1.0
        picks[REACH + i, breadth - REACH + i] = 1.0
    edges = lax.dot_general(
        jnp.asarray(picks, jnp.bfloat16),
        source_flux,
        (((1,), (2,)), ((), ())),
        preferred_element_type=jnp.float32,
    ).astype(jnp.bfloat16)
    beside = jnp.concatenate(neighbours(edges[:REACH], edges[REACH:], "blk", True), axis=0)
    rows = jnp.swapaxes(source_flux, 0, 1)
    above, below = neighbours(rows[:REACH], rows[height - REACH :], "panel", False)
    half = capacity // 2
    arrived = []
    for part, owners in enumerate(OWNERS):
        records = pl.pallas_call(
            functools.partial(record_body, start=part * half),
            grid_spec=pltpu.PrefetchScalarGridSpec(
                num_scalar_prefetch=1,
                grid=(members // owners,),
                in_specs=[
                    pl.BlockSpec((height, fields, breadth), lambda i, n: (0, 0, 0)),
                    pl.BlockSpec((REACH, fields, breadth), lambda i, n: (0, 0, 0)),
                    pl.BlockSpec((REACH, fields, breadth), lambda i, n: (0, 0, 0)),
                    pl.BlockSpec((2 * REACH, fields, height), lambda i, n: (0, 0, 0)),
                    pl.BlockSpec((points, members, half), lambda i, n, part=part: (0, 0, part)),
                    pl.BlockSpec(
                        (2, points, members, half), lambda i, n, part=part: (0, 0, 0, part)
                    ),
                    pl.BlockSpec((members, half), lambda i, n, part=part: (0, part)),
                ],
                out_specs=pl.BlockSpec((owners, fields, half), lambda i, n: (i, 0, 0)),
                scratch_shapes=[
                    pltpu.VMEM((groups * fields, span * breadth), jnp.bfloat16),
                    pltpu.VMEM((fields, 2 * REACH * height), jnp.bfloat16),
                    pltpu.VMEM((TERMS, members, half), jnp.float32),
                ],
            ),
            out_shape=jax.ShapeDtypeStruct((members, fields, half), jnp.bfloat16),
            name=f"records_{part}",
        )(
            slot_count,
            rows,
            above,
            below,
            beside,
            gauss_weight,
            gauss_offset,
            source_cell,
        )
        arrived.append(lax.all_to_all(records, "blk", split_axis=0, concat_axis=0, tiled=True))
    highs = cells // LOW
    padded = -(-fields // 16) * 16
    record_spec = pl.BlockSpec(memory_space=pltpu.VMEM)
    target_spec = pl.BlockSpec((members, capacity), lambda i: (0, 0))
    total_spec = pl.BlockSpec((highs * padded, LOW), lambda i: (0, 0))
    before = pl.pallas_call(
        functools.partial(deposit_first_body, highs=highs, padded=padded),
        grid=(members // BATCH,),
        in_specs=[record_spec, target_spec],
        out_specs=total_spec,
        out_shape=jax.ShapeDtypeStruct((highs * padded, LOW), jnp.float32),
        name="deposit_0",
    )(arrived[0], target_cell)
    return pl.pallas_call(
        functools.partial(deposit_last_body, highs=highs, padded=padded),
        grid=(members // BATCH,),
        in_specs=[
            record_spec,
            target_spec,
            total_spec,
            pl.BlockSpec((1, cells), lambda i: (0, 0)),
        ],
        out_specs=pl.BlockSpec((fields, cells), lambda i: (0, 0)),
        out_shape=jax.ShapeDtypeStruct((fields, cells), jnp.bfloat16),
        scratch_shapes=[pltpu.VMEM((highs * padded, LOW), jnp.float32)],
        name="deposit_1",
    )(arrived[1], target_cell, before, target_area.reshape(1, cells))


def solution(mesh):
    placed = (
        P(None, "panel", "blk"),
        P(None, ("panel", "blk"), None),
        P(None, None, ("panel", "blk"), None),
        P(("panel", "blk")),
        P(("panel", "blk"), None),
        P(("panel", "blk"), None),
        P(("panel", "blk")),
    )
    return jax.shard_map(
        on_device, mesh=mesh, in_specs=placed, out_specs=P(None, ("panel", "blk")), check_vma=False
    )
```

```python
import functools

import jax
import jax.numpy as jnp
import numpy as np
from jax import lax
from jax.experimental import pallas as pl
from jax.experimental.pallas import tpu as pltpu
from jax.sharding import PartitionSpec as P

GROUP = 8
REACH = 2
LOW = 256
TERMS = 11
OWNERS = (8, 4)


def slot_records(terms, window_ref, rim, *, fields, height, breadth):
    groups = height // GROUP
    span = GROUP + 2 * REACH
    slots = terms[0].shape[1]
    scale = terms[0]
    row_taps = terms[1:5]
    col_taps = terms[5:9]
    row = terms[9].astype(jnp.int32)
    col = terms[10].astype(jnp.int32)
    shifts = (-2, -1, 1, 2)
    group = row // GROUP
    local = row - group * GROUP + REACH
    one = jnp.ones((), jnp.bfloat16)
    zero = jnp.zeros((), jnp.bfloat16)
    place = lax.broadcasted_iota(jnp.int32, (breadth, slots), 0).astype(jnp.float32)
    gap = place.astype(jnp.bfloat16) - terms[10].astype(jnp.bfloat16)
    here = jnp.where(gap == 0, one, zero)
    beside = jnp.zeros((breadth, slots), jnp.bfloat16)
    for shift, tap in zip(shifts, col_taps):
        beside = jnp.where(gap == shift, tap.astype(jnp.bfloat16), beside)
    away = lax.broadcasted_iota(jnp.int32, (2 * GROUP, slots), 0) - local
    centres = jnp.where(away == 0, 1.0, 0.0)
    weights = centres
    for shift, tap in zip(shifts, row_taps):
        weights = jnp.where(away == shift, tap, weights)
    pieces = []
    for j in range(span):
        weight = weights[j : j + 1].astype(jnp.bfloat16)
        centre = centres[j : j + 1].astype(jnp.bfloat16)
        pieces.append(here * weight + beside * centre)
    table = jnp.concatenate(pieces, axis=0)
    product = jnp.dot(window_ref[...], table, preferred_element_type=jnp.float32)
    same_row = jnp.where(
        place[:height].astype(jnp.bfloat16) == terms[9].astype(jnp.bfloat16), one, zero
    )
    side = lax.broadcasted_iota(jnp.int32, (GROUP, slots), 0)
    reach = jnp.where(side < REACH, side - REACH, side + (breadth - REACH)) - col
    outer = jnp.zeros((GROUP, slots), jnp.float32)
    for shift, tap in zip(shifts, col_taps):
        outer = jnp.where(reach == shift, tap, outer)
    rim_pieces = [same_row * outer[i : i + 1].astype(jnp.bfloat16) for i in range(2 * REACH)]
    total = jnp.dot(rim, jnp.concatenate(rim_pieces, axis=0), preferred_element_type=jnp.float32)
    for g in range(groups):
        total = total + jnp.where(group == g, product[g * fields : (g + 1) * fields], 0.0)
    return (total * scale).astype(jnp.bfloat16)


def slot_terms(weight, offset, cell, count, *, start, breadth):
    offset_x = offset[0]
    offset_y = offset[1]
    slots = lax.broadcasted_iota(jnp.int32, cell.shape, 1) + start
    live = jnp.where(slots < count, 1.0, 0.0)
    area = jnp.sum(weight, axis=0)
    first_x = jnp.sum(weight * offset_x, axis=0)
    first_y = jnp.sum(weight * offset_y, axis=0)
    second_x = 0.5 * jnp.sum(weight * offset_x * offset_x, axis=0)
    second_y = 0.5 * jnp.sum(weight * offset_y * offset_y, axis=0)
    centre = area - 2.5 * (second_x + second_y)
    inverse = 1.0 / (12.0 * centre)
    terms = [centre * live]
    for one, two in ((first_x, second_x), (first_y, second_y)):
        terms += [
            (one - two) * inverse,
            (16.0 * two - 8.0 * one) * inverse,
            (16.0 * two + 8.0 * one) * inverse,
            (-one - two) * inverse,
        ]
    row = cell // breadth
    col = cell - row * breadth
    return terms + [row.astype(jnp.float32), col.astype(jnp.float32)]


def record_body(
    count_ref,
    rows_ref,
    above_ref,
    below_ref,
    beside_ref,
    weight_ref,
    offset_ref,
    cell_ref,
    out_ref,
    full_ref,
    rim_ref,
    term_ref,
    *,
    start,
):
    step = pl.program_id(0)
    height, fields, breadth = rows_ref.shape
    batch, _, slots = out_ref.shape

    @pl.when(step == 0)
    def fill():
        for g in range(height // GROUP):
            for j in range(GROUP + 2 * REACH):
                r = g * GROUP + j - REACH
                if r < 0:
                    part = above_ref[r + REACH]
                elif r >= height:
                    part = below_ref[r - height]
                else:
                    part = rows_ref[r]
                full_ref[g * fields : (g + 1) * fields, j * breadth : (j + 1) * breadth] = part
        rim_ref[...] = jnp.concatenate(
            [beside_ref[i] for i in range(2 * REACH)], axis=1
        )
        member = lax.broadcasted_iota(jnp.int32, cell_ref.shape, 0)
        count = jnp.zeros(cell_ref.shape, jnp.int32)
        for m in range(cell_ref.shape[0]):
            count = jnp.where(member == m, count_ref[m], count)
        terms = slot_terms(
            weight_ref[...],
            offset_ref[...],
            cell_ref[...],
            count,
            start=start,
            breadth=breadth,
        )
        for k, term in enumerate(terms):
            term_ref[k] = term

    rim = rim_ref[...]
    make = functools.partial(slot_records, fields=fields, height=height, breadth=breadth)
    take = lambda k, b: term_ref[k, pl.ds(step * batch + b, 1), :]
    if start == 0:
        terms = [
            jnp.concatenate([take(k, b) for b in range(batch)], axis=1) for k in range(TERMS)
        ]
        made = make(terms, full_ref, rim)
        for b in range(batch):
            out_ref[b] = made[:, b * slots : (b + 1) * slots]
    else:
        for b in range(batch):
            alive = count_ref[step * batch + b] > start

            @pl.when(alive)
            def compute():
                out_ref[b] = make([take(k, b) for k in range(TERMS)], full_ref, rim)

            @pl.when(jnp.logical_not(alive))
            def clear():
                out_ref[b] = jnp.zeros((fields, slots), out_ref.dtype)


def deposit_part(record_ref, target_ref, *, highs, padded, start):
    members, fields, half = record_ref.shape
    sources = range(members)
    target = jnp.concatenate(
        [target_ref[k : k + 1, start : start + half] for k in sources], axis=1
    )
    values = jnp.concatenate([record_ref[k] for k in sources], axis=1).astype(jnp.float32)
    slots = target.shape[1]
    values = jnp.concatenate(
        [values, jnp.zeros((padded - fields, slots), jnp.float32)], axis=0
    ).astype(jnp.bfloat16)
    high = target // LOW
    low = (target - high * LOW).astype(jnp.float32).astype(jnp.bfloat16)
    spread = jnp.concatenate(
        [values * jnp.where(high == h, 1.0, 0.0).astype(jnp.bfloat16) for h in range(highs)],
        axis=0,
    )
    lane = lax.broadcasted_iota(jnp.int32, (LOW, slots), 0).astype(jnp.float32)
    place = jnp.where(
        lane.astype(jnp.bfloat16) == low, jnp.ones((), jnp.bfloat16), jnp.zeros((), jnp.bfloat16)
    )
    return lax.dot_general(
        spread, place, (((1,), (1,)), ((), ())), preferred_element_type=jnp.float32
    )


def deposit_first_body(record_ref, target_ref, total_ref, *, highs, padded):
    total_ref[...] = deposit_part(record_ref, target_ref, highs=highs, padded=padded, start=0)


def deposit_last_body(record_ref, target_ref, before_ref, area_ref, out_ref, *, highs, padded):
    fields = out_ref.shape[0]
    part = deposit_part(
        record_ref, target_ref, highs=highs, padded=padded, start=record_ref.shape[2]
    )
    for h in range(highs):
        cut = slice(h * padded, h * padded + fields)
        inverse = 1.0 / area_ref[:, h * LOW : (h + 1) * LOW]
        out_ref[:, h * LOW : (h + 1) * LOW] = (
            (before_ref[cut, :] + part[cut]) * inverse
        ).astype(jnp.bfloat16)


def neighbours(first, last, axis, wrap):
    size = lax.axis_size(axis)
    up = [(i, (i + 1) % size) for i in range(size if wrap else size - 1)]
    down = [(j, i) for i, j in up]
    return (lax.ppermute(last, axis, up), lax.ppermute(first, axis, down))


def on_device(
    source_flux, gauss_weight, gauss_offset, slot_count, source_cell, target_cell, target_area
):
    fields, height, breadth = source_flux.shape
    members = lax.axis_size("blk")
    capacity = source_cell.shape[1]
    cells = target_area.shape[0]
    groups = height // GROUP
    span = GROUP + 2 * REACH
    points = gauss_weight.shape[0]
    picks = np.zeros((2 * REACH, breadth), np.float32)
    for i in range(REACH):
        picks[i, i] = 1.0
        picks[REACH + i, breadth - REACH + i] = 1.0
    edges = lax.dot_general(
        jnp.asarray(picks, jnp.bfloat16),
        source_flux,
        (((1,), (2,)), ((), ())),
        preferred_element_type=jnp.float32,
    ).astype(jnp.bfloat16)
    beside = jnp.concatenate(neighbours(edges[:REACH], edges[REACH:], "blk", True), axis=0)
    rows = jnp.swapaxes(source_flux, 0, 1)
    above, below = neighbours(rows[:REACH], rows[height - REACH :], "panel", False)
    half = capacity // 2
    arrived = []
    for part, owners in enumerate(OWNERS):
        records = pl.pallas_call(
            functools.partial(record_body, start=part * half),
            grid_spec=pltpu.PrefetchScalarGridSpec(
                num_scalar_prefetch=1,
                grid=(members // owners,),
                in_specs=[
                    pl.BlockSpec((height, fields, breadth), lambda i, n: (0, 0, 0)),
                    pl.BlockSpec((REACH, fields, breadth), lambda i, n: (0, 0, 0)),
                    pl.BlockSpec((REACH, fields, breadth), lambda i, n: (0, 0, 0)),
                    pl.BlockSpec((2 * REACH, fields, height), lambda i, n: (0, 0, 0)),
                    pl.BlockSpec((points, members, half), lambda i, n, part=part: (0, 0, part)),
                    pl.BlockSpec(
                        (2, points, members, half), lambda i, n, part=part: (0, 0, 0, part)
                    ),
                    pl.BlockSpec((members, half), lambda i, n, part=part: (0, part)),
                ],
                out_specs=pl.BlockSpec((owners, fields, half), lambda i, n: (i, 0, 0)),
                scratch_shapes=[
                    pltpu.VMEM((groups * fields, span * breadth), jnp.bfloat16),
                    pltpu.VMEM((fields, 2 * REACH * height), jnp.bfloat16),
                    pltpu.VMEM((TERMS, members, half), jnp.float32),
                ],
            ),
            out_shape=jax.ShapeDtypeStruct((members, fields, half), jnp.bfloat16),
            name=f"records_{part}",
        )(
            slot_count,
            rows,
            above,
            below,
            beside,
            gauss_weight,
            gauss_offset,
            source_cell,
        )
        arrived.append(lax.all_to_all(records, "blk", split_axis=0, concat_axis=0, tiled=True))
    highs = cells // LOW
    padded = -(-fields // 16) * 16
    record_spec = pl.BlockSpec(memory_space=pltpu.VMEM)
    target_spec = pl.BlockSpec((members, capacity), lambda i: (0, 0))
    total_spec = pl.BlockSpec((highs * padded, LOW), lambda i: (0, 0))
    before = pl.pallas_call(
        functools.partial(deposit_first_body, highs=highs, padded=padded),
        grid=(1,),
        in_specs=[record_spec, target_spec],
        out_specs=total_spec,
        out_shape=jax.ShapeDtypeStruct((highs * padded, LOW), jnp.float32),
        name="deposit_0",
    )(arrived[0], target_cell)
    return pl.pallas_call(
        functools.partial(deposit_last_body, highs=highs, padded=padded),
        grid=(1,),
        in_specs=[
            record_spec,
            target_spec,
            total_spec,
            pl.BlockSpec((1, cells), lambda i: (0, 0)),
        ],
        out_specs=pl.BlockSpec((fields, cells), lambda i: (0, 0)),
        out_shape=jax.ShapeDtypeStruct((fields, cells), jnp.bfloat16),
        name="deposit_1",
    )(arrived[1], target_cell, before, target_area.reshape(1, cells))


def solution(mesh):
    placed = (
        P(None, "panel", "blk"),
        P(None, ("panel", "blk"), None),
        P(None, None, ("panel", "blk"), None),
        P(("panel", "blk")),
        P(("panel", "blk"), None),
        P(("panel", "blk"), None),
        P(("panel", "blk")),
    )
    return jax.shard_map(
        on_device, mesh=mesh, in_specs=placed, out_specs=P(None, ("panel", "blk")), check_vma=False
    )
```

```python
import functools

import jax
import jax.numpy as jnp
import numpy as np
from jax import lax
from jax.experimental import pallas as pl
from jax.experimental.pallas import tpu as pltpu
from jax.sharding import PartitionSpec as P

GROUP = 8
REACH = 2
LOW = 256
TERMS = 11
OWNERS = (16, 4)


def slot_records(terms, window_ref, rim, *, fields, height, breadth):
    groups = height // GROUP
    span = GROUP + 2 * REACH
    slots = terms[0].shape[1]
    scale = terms[0]
    row_taps = terms[1:5]
    col_taps = terms[5:9]
    row = terms[9].astype(jnp.int32)
    col = terms[10].astype(jnp.int32)
    shifts = (-2, -1, 1, 2)
    group = row // GROUP
    local = row - group * GROUP + REACH
    one = jnp.ones((), jnp.bfloat16)
    zero = jnp.zeros((), jnp.bfloat16)
    place = lax.broadcasted_iota(jnp.int32, (breadth, slots), 0).astype(jnp.float32)
    gap = place.astype(jnp.bfloat16) - terms[10].astype(jnp.bfloat16)
    here = jnp.where(gap == 0, one, zero)
    beside = jnp.zeros((breadth, slots), jnp.bfloat16)
    for shift, tap in zip(shifts, col_taps):
        beside = jnp.where(gap == shift, tap.astype(jnp.bfloat16), beside)
    away = lax.broadcasted_iota(jnp.int32, (2 * GROUP, slots), 0) - local
    centres = jnp.where(away == 0, 1.0, 0.0)
    weights = centres
    for shift, tap in zip(shifts, row_taps):
        weights = jnp.where(away == shift, tap, weights)
    pieces = []
    for j in range(span):
        weight = weights[j : j + 1].astype(jnp.bfloat16)
        centre = centres[j : j + 1].astype(jnp.bfloat16)
        pieces.append(here * weight + beside * centre)
    table = jnp.concatenate(pieces, axis=0)
    product = jnp.dot(window_ref[...], table, preferred_element_type=jnp.float32)
    same_row = jnp.where(
        place[:height].astype(jnp.bfloat16) == terms[9].astype(jnp.bfloat16), one, zero
    )
    side = lax.broadcasted_iota(jnp.int32, (GROUP, slots), 0)
    reach = jnp.where(side < REACH, side - REACH, side + (breadth - REACH)) - col
    outer = jnp.zeros((GROUP, slots), jnp.float32)
    for shift, tap in zip(shifts, col_taps):
        outer = jnp.where(reach == shift, tap, outer)
    rim_pieces = [same_row * outer[i : i + 1].astype(jnp.bfloat16) for i in range(2 * REACH)]
    total = jnp.dot(rim, jnp.concatenate(rim_pieces, axis=0), preferred_element_type=jnp.float32)
    for g in range(groups):
        total = total + jnp.where(group == g, product[g * fields : (g + 1) * fields], 0.0)
    return (total * scale).astype(jnp.bfloat16)


def slot_terms(weight, offset, cell, count, *, start, breadth):
    offset_x = offset[0]
    offset_y = offset[1]
    slots = lax.broadcasted_iota(jnp.int32, cell.shape, 1) + start
    live = jnp.where(slots < count, 1.0, 0.0)
    area = jnp.sum(weight, axis=0)
    first_x = jnp.sum(weight * offset_x, axis=0)
    first_y = jnp.sum(weight * offset_y, axis=0)
    second_x = 0.5 * jnp.sum(weight * offset_x * offset_x, axis=0)
    second_y = 0.5 * jnp.sum(weight * offset_y * offset_y, axis=0)
    centre = area - 2.5 * (second_x + second_y)
    inverse = 1.0 / (12.0 * centre)
    terms = [centre * live]
    for one, two in ((first_x, second_x), (first_y, second_y)):
        terms += [
            (one - two) * inverse,
            (16.0 * two - 8.0 * one) * inverse,
            (16.0 * two + 8.0 * one) * inverse,
            (-one - two) * inverse,
        ]
    row = cell // breadth
    col = cell - row * breadth
    return terms + [row.astype(jnp.float32), col.astype(jnp.float32)]


def record_body(
    count_ref,
    rows_ref,
    above_ref,
    below_ref,
    beside_ref,
    weight_ref,
    offset_ref,
    cell_ref,
    out_ref,
    full_ref,
    rim_ref,
    term_ref,
    *,
    start,
):
    step = pl.program_id(0)
    height, fields, breadth = rows_ref.shape
    batch, _, slots = out_ref.shape

    @pl.when(step == 0)
    def fill():
        for g in range(height // GROUP):
            for j in range(GROUP + 2 * REACH):
                r = g * GROUP + j - REACH
                if r < 0:
                    part = above_ref[r + REACH]
                elif r >= height:
                    part = below_ref[r - height]
                else:
                    part = rows_ref[r]
                full_ref[g * fields : (g + 1) * fields, j * breadth : (j + 1) * breadth] = part
        rim_ref[...] = jnp.concatenate(
            [beside_ref[i] for i in range(2 * REACH)], axis=1
        )
        member = lax.broadcasted_iota(jnp.int32, cell_ref.shape, 0)
        count = jnp.zeros(cell_ref.shape, jnp.int32)
        for m in range(cell_ref.shape[0]):
            count = jnp.where(member == m, count_ref[m], count)
        terms = slot_terms(
            weight_ref[...],
            offset_ref[...],
            cell_ref[...],
            count,
            start=start,
            breadth=breadth,
        )
        for k, term in enumerate(terms):
            term_ref[k] = term

    rim = rim_ref[...]
    make = functools.partial(slot_records, fields=fields, height=height, breadth=breadth)
    take = lambda k, b: term_ref[k, pl.ds(step * batch + b, 1), :]
    if start == 0:
        terms = [
            jnp.concatenate([take(k, b) for b in range(batch)], axis=1) for k in range(TERMS)
        ]
        made = make(terms, full_ref, rim)
        for b in range(batch):
            out_ref[b] = made[:, b * slots : (b + 1) * slots]
    else:
        for b in range(batch):
            alive = count_ref[step * batch + b] > start

            @pl.when(alive)
            def compute():
                out_ref[b] = make([take(k, b) for k in range(TERMS)], full_ref, rim)

            @pl.when(jnp.logical_not(alive))
            def clear():
                out_ref[b] = jnp.zeros((fields, slots), out_ref.dtype)


def deposit_part(record_ref, target_ref, *, highs, padded, start):
    members, fields, half = record_ref.shape
    sources = range(members)
    target = jnp.concatenate(
        [target_ref[k : k + 1, start : start + half] for k in sources], axis=1
    )
    values = jnp.concatenate([record_ref[k] for k in sources], axis=1).astype(jnp.float32)
    slots = target.shape[1]
    values = jnp.concatenate(
        [values, jnp.zeros((padded - fields, slots), jnp.float32)], axis=0
    ).astype(jnp.bfloat16)
    high = target // LOW
    low = (target - high * LOW).astype(jnp.float32).astype(jnp.bfloat16)
    spread = jnp.concatenate(
        [values * jnp.where(high == h, 1.0, 0.0).astype(jnp.bfloat16) for h in range(highs)],
        axis=0,
    )
    lane = lax.broadcasted_iota(jnp.int32, (LOW, slots), 0).astype(jnp.float32)
    place = jnp.where(
        lane.astype(jnp.bfloat16) == low, jnp.ones((), jnp.bfloat16), jnp.zeros((), jnp.bfloat16)
    )
    return lax.dot_general(
        spread, place, (((1,), (1,)), ((), ())), preferred_element_type=jnp.float32
    )


def deposit_first_body(record_ref, target_ref, total_ref, *, highs, padded):
    total_ref[...] = deposit_part(record_ref, target_ref, highs=highs, padded=padded, start=0)


def deposit_last_body(record_ref, target_ref, before_ref, area_ref, out_ref, *, highs, padded):
    fields = out_ref.shape[0]
    part = deposit_part(
        record_ref, target_ref, highs=highs, padded=padded, start=record_ref.shape[2]
    )
    for h in range(highs):
        cut = slice(h * padded, h * padded + fields)
        inverse = 1.0 / area_ref[:, h * LOW : (h + 1) * LOW]
        out_ref[:, h * LOW : (h + 1) * LOW] = (
            (before_ref[cut, :] + part[cut]) * inverse
        ).astype(jnp.bfloat16)


def neighbours(first, last, axis, wrap):
    size = lax.axis_size(axis)
    up = [(i, (i + 1) % size) for i in range(size if wrap else size - 1)]
    down = [(j, i) for i, j in up]
    return (lax.ppermute(last, axis, up), lax.ppermute(first, axis, down))


def on_device(
    source_flux, gauss_weight, gauss_offset, slot_count, source_cell, target_cell, target_area
):
    fields, height, breadth = source_flux.shape
    members = lax.axis_size("blk")
    capacity = source_cell.shape[1]
    cells = target_area.shape[0]
    groups = height // GROUP
    span = GROUP + 2 * REACH
    points = gauss_weight.shape[0]
    picks = np.zeros((2 * REACH, breadth), np.float32)
    for i in range(REACH):
        picks[i, i] = 1.0
        picks[REACH + i, breadth - REACH + i] = 1.0
    edges = lax.dot_general(
        jnp.asarray(picks, jnp.bfloat16),
        source_flux,
        (((1,), (2,)), ((), ())),
        preferred_element_type=jnp.float32,
    ).astype(jnp.bfloat16)
    beside = jnp.concatenate(neighbours(edges[:REACH], edges[REACH:], "blk", True), axis=0)
    rows = jnp.swapaxes(source_flux, 0, 1)
    above, below = neighbours(rows[:REACH], rows[height - REACH :], "panel", False)
    half = capacity // 2
    arrived = []
    for part, owners in enumerate(OWNERS):
        records = pl.pallas_call(
            functools.partial(record_body, start=part * half),
            grid_spec=pltpu.PrefetchScalarGridSpec(
                num_scalar_prefetch=1,
                grid=(members // owners,),
                in_specs=[
                    pl.BlockSpec((height, fields, breadth), lambda i, n: (0, 0, 0)),
                    pl.BlockSpec((REACH, fields, breadth), lambda i, n: (0, 0, 0)),
                    pl.BlockSpec((REACH, fields, breadth), lambda i, n: (0, 0, 0)),
                    pl.BlockSpec((2 * REACH, fields, height), lambda i, n: (0, 0, 0)),
                    pl.BlockSpec((points, members, half), lambda i, n, part=part: (0, 0, part)),
                    pl.BlockSpec(
                        (2, points, members, half), lambda i, n, part=part: (0, 0, 0, part)
                    ),
                    pl.BlockSpec((members, half), lambda i, n, part=part: (0, part)),
                ],
                out_specs=pl.BlockSpec((owners, fields, half), lambda i, n: (i, 0, 0)),
                scratch_shapes=[
                    pltpu.VMEM((groups * fields, span * breadth), jnp.bfloat16),
                    pltpu.VMEM((fields, 2 * REACH * height), jnp.bfloat16),
                    pltpu.VMEM((TERMS, members, half), jnp.float32),
                ],
            ),
            out_shape=jax.ShapeDtypeStruct((members, fields, half), jnp.bfloat16),
            name=f"records_{part}",
        )(
            slot_count,
            rows,
            above,
            below,
            beside,
            gauss_weight,
            gauss_offset,
            source_cell,
        )
        arrived.append(lax.all_to_all(records, "blk", split_axis=0, concat_axis=0, tiled=True))
    highs = cells // LOW
    padded = -(-fields // 16) * 16
    record_spec = pl.BlockSpec(memory_space=pltpu.VMEM)
    target_spec = pl.BlockSpec((members, capacity), lambda i: (0, 0))
    total_spec = pl.BlockSpec((highs * padded, LOW), lambda i: (0, 0))
    before = pl.pallas_call(
        functools.partial(deposit_first_body, highs=highs, padded=padded),
        grid=(1,),
        in_specs=[record_spec, target_spec],
        out_specs=total_spec,
        out_shape=jax.ShapeDtypeStruct((highs * padded, LOW), jnp.float32),
        name="deposit_0",
    )(arrived[0], target_cell)
    return pl.pallas_call(
        functools.partial(deposit_last_body, highs=highs, padded=padded),
        grid=(1,),
        in_specs=[
            record_spec,
            target_spec,
            total_spec,
            pl.BlockSpec((1, cells), lambda i: (0, 0)),
        ],
        out_specs=pl.BlockSpec((fields, cells), lambda i: (0, 0)),
        out_shape=jax.ShapeDtypeStruct((fields, cells), jnp.bfloat16),
        name="deposit_1",
    )(arrived[1], target_cell, before, target_area.reshape(1, cells))


def solution(mesh):
    placed = (
        P(None, "panel", "blk"),
        P(None, ("panel", "blk"), None),
        P(None, None, ("panel", "blk"), None),
        P(("panel", "blk")),
        P(("panel", "blk"), None),
        P(("panel", "blk"), None),
        P(("panel", "blk")),
    )
    return jax.shard_map(
        on_device, mesh=mesh, in_specs=placed, out_specs=P(None, ("panel", "blk")), check_vma=False
    )
```

```python
import functools

import jax
import jax.numpy as jnp
import numpy as np
from jax import lax
from jax.experimental import pallas as pl
from jax.experimental.pallas import tpu as pltpu
from jax.sharding import PartitionSpec as P

GROUP = 8
REACH = 2
LOW = 256
TERMS = 11
OWNERS = (8, 8)


def slot_records(terms, window_ref, rim, *, fields, height, breadth):
    groups = height // GROUP
    span = GROUP + 2 * REACH
    slots = terms[0].shape[1]
    scale = terms[0]
    row_taps = terms[1:5]
    col_taps = terms[5:9]
    row = terms[9].astype(jnp.int32)
    col = terms[10].astype(jnp.int32)
    shifts = (-2, -1, 1, 2)
    group = row // GROUP
    local = row - group * GROUP + REACH
    one = jnp.ones((), jnp.bfloat16)
    zero = jnp.zeros((), jnp.bfloat16)
    place = lax.broadcasted_iota(jnp.int32, (breadth, slots), 0).astype(jnp.float32)
    gap = place.astype(jnp.bfloat16) - terms[10].astype(jnp.bfloat16)
    here = jnp.where(gap == 0, one, zero)
    beside = jnp.zeros((breadth, slots), jnp.bfloat16)
    for shift, tap in zip(shifts, col_taps):
        beside = jnp.where(gap == shift, tap.astype(jnp.bfloat16), beside)
    away = lax.broadcasted_iota(jnp.int32, (2 * GROUP, slots), 0) - local
    centres = jnp.where(away == 0, 1.0, 0.0)
    weights = centres
    for shift, tap in zip(shifts, row_taps):
        weights = jnp.where(away == shift, tap, weights)
    pieces = []
    for j in range(span):
        weight = weights[j : j + 1].astype(jnp.bfloat16)
        centre = centres[j : j + 1].astype(jnp.bfloat16)
        pieces.append(here * weight + beside * centre)
    table = jnp.concatenate(pieces, axis=0)
    product = jnp.dot(window_ref[...], table, preferred_element_type=jnp.float32)
    same_row = jnp.where(
        place[:height].astype(jnp.bfloat16) == terms[9].astype(jnp.bfloat16), one, zero
    )
    side = lax.broadcasted_iota(jnp.int32, (GROUP, slots), 0)
    reach = jnp.where(side < REACH, side - REACH, side + (breadth - REACH)) - col
    outer = jnp.zeros((GROUP, slots), jnp.float32)
    for shift, tap in zip(shifts, col_taps):
        outer = jnp.where(reach == shift, tap, outer)
    rim_pieces = [same_row * outer[i : i + 1].astype(jnp.bfloat16) for i in range(2 * REACH)]
    total = jnp.dot(rim, jnp.concatenate(rim_pieces, axis=0), preferred_element_type=jnp.float32)
    for g in range(groups):
        total = total + jnp.where(group == g, product[g * fields : (g + 1) * fields], 0.0)
    return (total * scale).astype(jnp.bfloat16)


def slot_terms(weight, offset, cell, count, *, start, breadth):
    offset_x = offset[0]
    offset_y = offset[1]
    slots = lax.broadcasted_iota(jnp.int32, cell.shape, 1) + start
    live = jnp.where(slots < count, 1.0, 0.0)
    area = jnp.sum(weight, axis=0)
    first_x = jnp.sum(weight * offset_x, axis=0)
    first_y = jnp.sum(weight * offset_y, axis=0)
    second_x = 0.5 * jnp.sum(weight * offset_x * offset_x, axis=0)
    second_y = 0.5 * jnp.sum(weight * offset_y * offset_y, axis=0)
    centre = area - 2.5 * (second_x + second_y)
    inverse = 1.0 / (12.0 * centre)
    terms = [centre * live]
    for one, two in ((first_x, second_x), (first_y, second_y)):
        terms += [
            (one - two) * inverse,
            (16.0 * two - 8.0 * one) * inverse,
            (16.0 * two + 8.0 * one) * inverse,
            (-one - two) * inverse,
        ]
    row = cell // breadth
    col = cell - row * breadth
    return terms + [row.astype(jnp.float32), col.astype(jnp.float32)]


def record_body(
    count_ref,
    rows_ref,
    above_ref,
    below_ref,
    beside_ref,
    weight_ref,
    offset_ref,
    cell_ref,
    out_ref,
    full_ref,
    rim_ref,
    term_ref,
    *,
    start,
):
    step = pl.program_id(0)
    height, fields, breadth = rows_ref.shape
    batch, _, slots = out_ref.shape

    @pl.when(step == 0)
    def fill():
        for g in range(height // GROUP):
            for j in range(GROUP + 2 * REACH):
                r = g * GROUP + j - REACH
                if r < 0:
                    part = above_ref[r + REACH]
                elif r >= height:
                    part = below_ref[r - height]
                else:
                    part = rows_ref[r]
                full_ref[g * fields : (g + 1) * fields, j * breadth : (j + 1) * breadth] = part
        rim_ref[...] = jnp.concatenate(
            [beside_ref[i] for i in range(2 * REACH)], axis=1
        )
        member = lax.broadcasted_iota(jnp.int32, cell_ref.shape, 0)
        count = jnp.zeros(cell_ref.shape, jnp.int32)
        for m in range(cell_ref.shape[0]):
            count = jnp.where(member == m, count_ref[m], count)
        terms = slot_terms(
            weight_ref[...],
            offset_ref[...],
            cell_ref[...],
            count,
            start=start,
            breadth=breadth,
        )
        for k, term in enumerate(terms):
            term_ref[k] = term

    rim = rim_ref[...]
    make = functools.partial(slot_records, fields=fields, height=height, breadth=breadth)
    take = lambda k, b: term_ref[k, pl.ds(step * batch + b, 1), :]
    if start == 0:
        terms = [
            jnp.concatenate([take(k, b) for b in range(batch)], axis=1) for k in range(TERMS)
        ]
        made = make(terms, full_ref, rim)
        for b in range(batch):
            out_ref[b] = made[:, b * slots : (b + 1) * slots]
    else:
        for b in range(batch):
            alive = count_ref[step * batch + b] > start

            @pl.when(alive)
            def compute():
                out_ref[b] = make([take(k, b) for k in range(TERMS)], full_ref, rim)

            @pl.when(jnp.logical_not(alive))
            def clear():
                out_ref[b] = jnp.zeros((fields, slots), out_ref.dtype)


def deposit_part(record_ref, target_ref, *, highs, padded, start):
    members, fields, half = record_ref.shape
    sources = range(members)
    target = jnp.concatenate(
        [target_ref[k : k + 1, start : start + half] for k in sources], axis=1
    )
    values = jnp.concatenate([record_ref[k] for k in sources], axis=1).astype(jnp.float32)
    slots = target.shape[1]
    values = jnp.concatenate(
        [values, jnp.zeros((padded - fields, slots), jnp.float32)], axis=0
    ).astype(jnp.bfloat16)
    high = target // LOW
    low = (target - high * LOW).astype(jnp.float32).astype(jnp.bfloat16)
    spread = jnp.concatenate(
        [values * jnp.where(high == h, 1.0, 0.0).astype(jnp.bfloat16) for h in range(highs)],
        axis=0,
    )
    lane = lax.broadcasted_iota(jnp.int32, (LOW, slots), 0).astype(jnp.float32)
    place = jnp.where(
        lane.astype(jnp.bfloat16) == low, jnp.ones((), jnp.bfloat16), jnp.zeros((), jnp.bfloat16)
    )
    return lax.dot_general(
        spread, place, (((1,), (1,)), ((), ())), preferred_element_type=jnp.float32
    )


def deposit_first_body(record_ref, target_ref, total_ref, *, highs, padded):
    total_ref[...] = deposit_part(record_ref, target_ref, highs=highs, padded=padded, start=0)


def deposit_last_body(record_ref, target_ref, before_ref, area_ref, out_ref, *, highs, padded):
    fields = out_ref.shape[0]
    part = deposit_part(
        record_ref, target_ref, highs=highs, padded=padded, start=record_ref.shape[2]
    )
    for h in range(highs):
        cut = slice(h * padded, h * padded + fields)
        inverse = 1.0 / area_ref[:, h * LOW : (h + 1) * LOW]
        out_ref[:, h * LOW : (h + 1) * LOW] = (
            (before_ref[cut, :] + part[cut]) * inverse
        ).astype(jnp.bfloat16)


def neighbours(first, last, axis, wrap):
    size = lax.axis_size(axis)
    up = [(i, (i + 1) % size) for i in range(size if wrap else size - 1)]
    down = [(j, i) for i, j in up]
    return (lax.ppermute(last, axis, up), lax.ppermute(first, axis, down))


def on_device(
    source_flux, gauss_weight, gauss_offset, slot_count, source_cell, target_cell, target_area
):
    fields, height, breadth = source_flux.shape
    members = lax.axis_size("blk")
    capacity = source_cell.shape[1]
    cells = target_area.shape[0]
    groups = height // GROUP
    span = GROUP + 2 * REACH
    points = gauss_weight.shape[0]
    picks = np.zeros((2 * REACH, breadth), np.float32)
    for i in range(REACH):
        picks[i, i] = 1.0
        picks[REACH + i, breadth - REACH + i] = 1.0
    edges = lax.dot_general(
        jnp.asarray(picks, jnp.bfloat16),
        source_flux,
        (((1,), (2,)), ((), ())),
        preferred_element_type=jnp.float32,
    ).astype(jnp.bfloat16)
    beside = jnp.concatenate(neighbours(edges[:REACH], edges[REACH:], "blk", True), axis=0)
    rows = jnp.swapaxes(source_flux, 0, 1)
    above, below = neighbours(rows[:REACH], rows[height - REACH :], "panel", False)
    half = capacity // 2
    arrived = []
    for part, owners in enumerate(OWNERS):
        records = pl.pallas_call(
            functools.partial(record_body, start=part * half),
            grid_spec=pltpu.PrefetchScalarGridSpec(
                num_scalar_prefetch=1,
                grid=(members // owners,),
                in_specs=[
                    pl.BlockSpec((height, fields, breadth), lambda i, n: (0, 0, 0)),
                    pl.BlockSpec((REACH, fields, breadth), lambda i, n: (0, 0, 0)),
                    pl.BlockSpec((REACH, fields, breadth), lambda i, n: (0, 0, 0)),
                    pl.BlockSpec((2 * REACH, fields, height), lambda i, n: (0, 0, 0)),
                    pl.BlockSpec((points, members, half), lambda i, n, part=part: (0, 0, part)),
                    pl.BlockSpec(
                        (2, points, members, half), lambda i, n, part=part: (0, 0, 0, part)
                    ),
                    pl.BlockSpec((members, half), lambda i, n, part=part: (0, part)),
                ],
                out_specs=pl.BlockSpec((owners, fields, half), lambda i, n: (i, 0, 0)),
                scratch_shapes=[
                    pltpu.VMEM((groups * fields, span * breadth), jnp.bfloat16),
                    pltpu.VMEM((fields, 2 * REACH * height), jnp.bfloat16),
                    pltpu.VMEM((TERMS, members, half), jnp.float32),
                ],
            ),
            out_shape=jax.ShapeDtypeStruct((members, fields, half), jnp.bfloat16),
            name=f"records_{part}",
        )(
            slot_count,
            rows,
            above,
            below,
            beside,
            gauss_weight,
            gauss_offset,
            source_cell,
        )
        arrived.append(lax.all_to_all(records, "blk", split_axis=0, concat_axis=0, tiled=True))
    highs = cells // LOW
    padded = -(-fields // 16) * 16
    record_spec = pl.BlockSpec(memory_space=pltpu.VMEM)
    target_spec = pl.BlockSpec((members, capacity), lambda i: (0, 0))
    total_spec = pl.BlockSpec((highs * padded, LOW), lambda i: (0, 0))
    before = pl.pallas_call(
        functools.partial(deposit_first_body, highs=highs, padded=padded),
        grid=(1,),
        in_specs=[record_spec, target_spec],
        out_specs=total_spec,
        out_shape=jax.ShapeDtypeStruct((highs * padded, LOW), jnp.float32),
        name="deposit_0",
    )(arrived[0], target_cell)
    return pl.pallas_call(
        functools.partial(deposit_last_body, highs=highs, padded=padded),
        grid=(1,),
        in_specs=[
            record_spec,
            target_spec,
            total_spec,
            pl.BlockSpec((1, cells), lambda i: (0, 0)),
        ],
        out_specs=pl.BlockSpec((fields, cells), lambda i: (0, 0)),
        out_shape=jax.ShapeDtypeStruct((fields, cells), jnp.bfloat16),
        name="deposit_1",
    )(arrived[1], target_cell, before, target_area.reshape(1, cells))


def solution(mesh):
    placed = (
        P(None, "panel", "blk"),
        P(None, ("panel", "blk"), None),
        P(None, None, ("panel", "blk"), None),
        P(("panel", "blk")),
        P(("panel", "blk"), None),
        P(("panel", "blk"), None),
        P(("panel", "blk")),
    )
    return jax.shard_map(
        on_device, mesh=mesh, in_specs=placed, out_specs=P(None, ("panel", "blk")), check_vma=False
    )
```
